1024 devices in a mesh: section: 4 (over x), ctx: 16 (over y, core), exp: 16 (over z).
Axes of the slice: x: 4, y: 8, z: 16, core: 2. Of those that a mesh axis runs over, the one named last changes fastest.
Arguments:
- queries: bfloat16 [16384, 8192], P('ctx', ('section', 'exp')), may hold values from -6 to 6
- key_rows: bfloat16 [16384, 8192], P('ctx', ('section', 'exp')), may hold values from -0.5 to 0.5
- value_rows: bfloat16 [16384, 8192], P('ctx', ('section', 'exp')), may hold values from -6 to 6
- gate_input: bfloat16 [16384, 8192], P('ctx', ('section', 'exp')), may hold values from -6 to 6
- norm_gain: float32 [8192], P(('section', 'exp')), may hold values from 0.25 to 1.75
- log_decay: float32 [64, 16384], P(('section', 'exp'), 'ctx'), may hold values from -1 to 0, as said below
- grad_output: bfloat16 [16384, 8192], P('ctx', ('section', 'exp')), may hold values from -6 to 6
Outputs:
- layer_out: bfloat16 [16384, 8192], P('ctx', ('section', 'exp'))
- grad_queries: bfloat16 [16384, 8192], P('ctx', ('section', 'exp'))
- grad_keys: bfloat16 [16384, 8192], P('ctx', ('section', 'exp'))
- grad_values: bfloat16 [16384, 8192], P('ctx', ('section', 'exp'))
- grad_gate: bfloat16 [16384, 8192], P('ctx', ('section', 'exp'))
The draws below stay inside these ranges and needn't reach their ends.
Inputs may be any that keep to these rules, and one draw needn't show every extreme that they name: `log_decay`: each entry is the logarithm of one head's decay factor at one position.
All inputs are finite; a program needn't handle non-finite values.
Results may differ from the reference program's by a relative error of at most 0.0051.
Values sent between devices are 32-bit elements; how exact they have to be, the bound alone decides.
No kernel may reach another device: no remote copies, remote signals or barrier semaphores. Data moves between devices by JAX's collectives and lax.ppermute only.
A program may use at most 32 MiB of HBM per device.

```python
import math
import jax
import jax.numpy as jnp
from jax import lax

HEAD_DIM = 128
L_DEV = 1024
ATTENTION_COUNT = 64
TOKEN_SPAN = 16384


def draw_log_decay(key, part):
    keys_list = jax.random.split(jax.random.fold_in(key, 7101), 6)
    fast_share = 0.5
    is_fast = jax.random.uniform(keys_list[0], (ATTENTION_COUNT, 1)) < fast_share
    fast_rate = jnp.exp(jax.random.uniform(keys_list[1], (ATTENTION_COUNT, 1), jnp.float32, math.log(1.0 / 50.0), math.log(1.0 / 30.0)))
    slow_rate = jnp.exp(jax.random.uniform(keys_list[2], (ATTENTION_COUNT, 1), jnp.float32, math.log(0.1 / TOKEN_SPAN), math.log(0.6 / TOKEN_SPAN)))
    forgetting_factor = jnp.where(is_fast, fast_rate, slow_rate)
    approximate_guess = jax.random.uniform(keys_list[3], (ATTENTION_COUNT, TOKEN_SPAN), jnp.float32, 0.5, 2.0)
    location_array = jax.random.randint(keys_list[4], (ATTENTION_COUNT, 3), 0, TOKEN_SPAN)
    network_level = jnp.log(jax.random.uniform(keys_list[5], (ATTENTION_COUNT, 3), jnp.float32, 0.5, 0.8))
    matrix_field = jax.lax.broadcasted_iota(jnp.int32, (ATTENTION_COUNT, TOKEN_SPAN), 1)
    tile_batches = jnp.zeros((ATTENTION_COUNT, TOKEN_SPAN), jnp.float32)
    for picker_ordinal in range(3):
        tile_batches = tile_batches + jnp.where(matrix_field == location_array[:, picker_ordinal:picker_ordinal + 1], network_level[:, picker_ordinal:picker_ordinal + 1], 0.0)
    return (-forgetting_factor * approximate_guess + tile_batches).astype(jnp.float32)


def steps_of(own_key, dims, shards, low, high):
    factor_of = 1.0
    for position, blocks in shards:
        draws = jax.random.uniform(jax.random.fold_in(jax.random.fold_in(own_key, 6), position), (blocks,), jnp.float32, low / len(shards), high / len(shards))
        factor_of = factor_of * jnp.repeat(jnp.exp(draws), dims[position] // blocks).reshape((-1,) + (1,) * (len(dims) - 1 - position))
    return factor_of


def normal_values(rng, dims, spread, limit, cuts=(), held_as=jnp.bfloat16):
    array = spread * jax.random.normal(rng, dims, jnp.float32)
    if cuts:
        array = array * steps_of(rng, dims, cuts, -0.22, 0.18)
    return jnp.clip(array, -limit, limit).astype(held_as)


def setup_inputs(seed: int = 0) -> dict:
    arg_keys = jax.random.split(jax.random.key(seed), 8)
    queries = normal_values(arg_keys[0], (TOKEN_SPAN, ATTENTION_COUNT * HEAD_DIM), 1.0, 6.0, ((0, 16), (1, 64)))
    key_rows = normal_values(arg_keys[1], (TOKEN_SPAN, ATTENTION_COUNT * HEAD_DIM), HEAD_DIM ** -0.5, 0.5, ((0, 16), (1, 64)))
    value_rows = normal_values(arg_keys[2], (TOKEN_SPAN, ATTENTION_COUNT * HEAD_DIM), 1.0, 6.0, ((0, 16), (1, 64)))
    gate_input = normal_values(arg_keys[3], (TOKEN_SPAN, ATTENTION_COUNT * HEAD_DIM), 1.0, 6.0, ((0, 16), (1, 64)))
    norm_gain = jnp.clip(1.0 + 0.15 * jax.random.normal(arg_keys[4], (ATTENTION_COUNT * HEAD_DIM,), jnp.float32), 0.25, 1.75)
    log_decay = draw_log_decay(jax.random.fold_in(arg_keys[7], 71), 0)
    grad_output = normal_values(arg_keys[6], (TOKEN_SPAN, ATTENTION_COUNT * HEAD_DIM), 1.0, 6.0, ((0, 16), (1, 64)))
    return dict(queries=queries, key_rows=key_rows, value_rows=value_rows, gate_input=gate_input, norm_gain=norm_gain, log_decay=log_decay, grad_output=grad_output)


precise = lax.Precision.HIGHEST
epsilon = 1e-06

def decay_weights(log_rates):
    cumulated = jnp.cumsum(log_rates)
    length = log_rates.shape[0]
    row_index = lax.broadcasted_iota(jnp.int32, (length, length), 0)
    col_index = lax.broadcasted_iota(jnp.int32, (length, length), 1)
    lower = jnp.exp(jnp.minimum(cumulated[:, None] - cumulated[None, :], 0.0))
    return (cumulated, jnp.where(row_index >= col_index, lower, 0.0))

def block_forward(entering, pieces):
    queries, key_rows, value_rows, log_rates = pieces
    cumulated, weights_table = decay_weights(log_rates)
    scores = jnp.dot(queries, key_rows.T, preferred_element_type=jnp.float32)
    weights = (scores * weights_table).astype(jnp.bfloat16)
    carried = jnp.dot(queries.astype(jnp.float32), entering, precision=precise)
    output = jnp.dot(weights, value_rows, preferred_element_type=jnp.float32) + jnp.exp(cumulated)[:, None] * carried
    tail_decay = jnp.exp(cumulated[-1] - cumulated)[:, None]
    update = jnp.dot((key_rows.astype(jnp.float32) * tail_decay).T, value_rows.astype(jnp.float32), precision=precise)
    leaving = jnp.exp(cumulated[-1]) * entering + update
    return (leaving, (output, entering))

def split_blocks(tensor, block_len):
    return tensor.reshape((tensor.shape[0] // block_len, block_len) + tensor.shape[1:])

def forward_run(queries, key_rows, value_rows, log_rates, start, block_len):
    pieces = tuple((split_blocks(t, block_len) for t in (queries, key_rows, value_rows, log_rates)))
    closing, (outputs, entries) = lax.scan(block_forward, start, pieces)
    return (outputs.reshape(queries.shape), entries, closing)

def block_backward(leaving, pieces):
    queries, key_rows, value_rows, grad_attn, log_rates, entering = pieces
    cumulated, weights_table = decay_weights(log_rates)
    qk_weights = (jnp.dot(queries, key_rows.T, preferred_element_type=jnp.float32) * weights_table).astype(jnp.bfloat16)
    dv_weights = (jnp.dot(grad_attn, value_rows.T, preferred_element_type=jnp.float32) * weights_table).astype(jnp.bfloat16)
    front_decay = jnp.exp(cumulated)[:, None]
    tail_decay = jnp.exp(cumulated[-1] - cumulated)[:, None]
    grad_float = grad_attn.astype(jnp.float32)
    grad_q = jnp.dot(dv_weights, key_rows, preferred_element_type=jnp.float32) + front_decay * jnp.dot(grad_float, entering.T, precision=precise)
    grad_k = jnp.dot(dv_weights.T, queries, preferred_element_type=jnp.float32) + tail_decay * jnp.dot(value_rows.astype(jnp.float32), leaving.T, precision=precise)
    grad_v = jnp.dot(qk_weights.T, grad_attn, preferred_element_type=jnp.float32) + tail_decay * jnp.dot(key_rows.astype(jnp.float32), leaving, precision=precise)
    arriving = jnp.exp(cumulated[-1]) * leaving + jnp.dot((queries.astype(jnp.float32) * front_decay).T, grad_float, precision=precise)
    return (arriving, (grad_q, grad_k, grad_v))

def backward_run(queries, key_rows, value_rows, grad_attn, log_rates, entries, start, block_len):
    pieces = tuple((split_blocks(t, block_len) for t in (queries, key_rows, value_rows, grad_attn, log_rates))) + (entries,)
    closing, (grad_q, grad_k, grad_v) = lax.scan(block_backward, start, pieces, reverse=True)
    shape = queries.shape
    return (grad_q.reshape(shape), grad_k.reshape(shape), grad_v.reshape(shape), closing)

def by_heads(tensor, head_count):
    return tensor.reshape(tensor.shape[0], head_count, HEAD_DIM).transpose(1, 0, 2)

def from_heads(tensor):
    return tensor.transpose(1, 0, 2).reshape(tensor.shape[1], tensor.shape[0] * tensor.shape[2])

def reference(queries, key_rows, value_rows, gate_input, norm_gain, log_decay, grad_output):
    block_len = min(512, L_DEV)
    head_count = log_decay.shape[0]
    total_width = head_count * HEAD_DIM
    zero_state = jnp.zeros((HEAD_DIM, HEAD_DIM), jnp.float32)
    query_heads = by_heads(queries, head_count)
    key_heads = by_heads(key_rows, head_count)
    value_heads = by_heads(value_rows, head_count)

    def forward_head(items):
        outputs, entries, closing = forward_run(items[0], items[1], items[2], items[3], zero_state, block_len)
        return (outputs, entries)
    attn_heads, entries = lax.map(forward_head, (query_heads, key_heads, value_heads, log_decay))
    full_out = from_heads(attn_heads)
    squares = lax.optimization_barrier(jnp.sum(full_out * full_out, axis=1))
    inv_rms = lax.rsqrt(squares / total_width + epsilon)
    normed = full_out * inv_rms[:, None]
    gate_prob = jax.nn.sigmoid(gate_input.astype(jnp.float32))
    scaled = normed * norm_gain
    layer_out = (scaled * gate_prob).astype(jnp.bfloat16)
    grad_float = grad_output.astype(jnp.float32)
    grad_gate = (grad_float * scaled * gate_prob * (1.0 - gate_prob)).astype(jnp.bfloat16)
    signal = grad_float * gate_prob * norm_gain
    along = lax.optimization_barrier(jnp.sum(signal * normed, axis=1)) / total_width
    grad_attn = (inv_rms[:, None] * (signal - normed * along[:, None])).astype(jnp.bfloat16)
    grad_heads = by_heads(grad_attn, head_count)

    def backward_head(items):
        grad_q, grad_k, grad_v, closing = backward_run(items[0], items[1], items[2], items[3], items[4], items[5], zero_state, block_len)
        return (grad_q, grad_k, grad_v)
    grad_q, grad_k, grad_v = lax.map(backward_head, (query_heads, key_heads, value_heads, grad_heads, log_decay, entries))
    return (layer_out, from_heads(grad_q).astype(jnp.bfloat16), from_heads(grad_k).astype(jnp.bfloat16), from_heads(grad_v).astype(jnp.bfloat16), grad_gate)
```

```python
from functools import partial

import jax
import jax.numpy as jnp
from jax import lax
from jax.experimental import pallas as pl
from jax.experimental.pallas import tpu as pltpu
from jax.sharding import PartitionSpec as P

HEAD_DIM = 128
BLOCK = 512
TILE = 256
CHUNK = 128
EPSILON = 1e-06
f32 = jnp.float32
bf16 = jnp.bfloat16


def dot(a, b, ca=1, cb=0):
    return lax.dot_general(a, b, (((ca,), (cb,)), ((), ())), preferred_element_type=f32)


def split3(x):
    hi = x.astype(bf16)
    rest = x - hi.astype(f32)
    mid = rest.astype(bf16)
    return hi, mid, (rest - mid.astype(f32)).astype(bf16)


def exact_dot(a, b, ca=1, cb=0):
    hi, mid, lo = split3(b)
    return dot(a, hi, ca, cb) + (dot(a, mid, ca, cb) + dot(a, lo, ca, cb))


def cumulate(rates):
    rows = rates.shape[0]
    per_block = BLOCK // CHUNK
    r = lax.broadcasted_iota(jnp.int32, (CHUNK, CHUNK), 0)
    c = lax.broadcasted_iota(jnp.int32, (CHUNK, CHUNK), 1)
    upper = jnp.where(r <= c, 1.0, 0.0).astype(bf16)
    hi, mid, lo = split3(rates)
    within = dot(hi, upper) + (dot(mid, upper) + dot(lo, upper))
    total = within[:, CHUNK - 1 :]
    pieces = []
    for row in range(rows):
        value = within[row : row + 1, :]
        for earlier in range(row // per_block * per_block, row):
            value = value + total[earlier : earlier + 1, :]
        pieces.append(value)
    return jnp.concatenate(pieces, axis=0)


def column(turned, first, count):
    return jnp.concatenate(
        [turned[:, r : r + 1] for r in range(first // CHUNK, (first + count) // CHUNK)], axis=0
    )


def row_of(sums, first, count):
    return jnp.concatenate(
        [sums[r : r + 1, :] for r in range(first // CHUNK, (first + count) // CHUNK)], axis=1
    )


def last_of(sums, block):
    row = (block + 1) * BLOCK // CHUNK - 1
    return sums[row : row + 1, CHUNK - 1 :]


def weights_tile(sums, turned, start, tile):
    first = start + tile * TILE
    width = (tile + 1) * TILE
    gap = column(turned, first, TILE) - row_of(sums, start, width)
    lower = jnp.exp(jnp.minimum(gap, 0.0))
    t = lax.broadcasted_iota(jnp.int32, (TILE, width), 0) + tile * TILE
    s = lax.broadcasted_iota(jnp.int32, (TILE, width), 1)
    return jnp.where(t >= s, lower, 0.0)


def states_kernel(n_ctx, k_ref, v_ref, rates_ref, send_ref, entry_ref, sums_ref, turned_ref):
    length = k_ref.shape[0]
    blocks = length // BLOCK
    sums = cumulate(rates_ref[...])
    turned = sums.T
    sums_ref[...] = sums
    turned_ref[...] = turned
    state = None
    total = jnp.zeros((1, 1), f32)
    for b in range(blocks):
        at = b * BLOCK
        last = last_of(sums, b)
        tail = jnp.exp(last - column(turned, at, BLOCK))
        scaled = v_ref[at : at + BLOCK, :].astype(f32) * tail
        update = exact_dot(k_ref[at : at + BLOCK, :], scaled, 0, 0)
        state = update if state is None else jnp.exp(last) * state + update
        total = total + last
        if b < blocks - 1:
            entry_ref[b] = state
    rows = HEAD_DIM // n_ctx
    spread = jnp.broadcast_to(total, (rows, HEAD_DIM))
    for j in range(n_ctx):
        send_ref[j, :rows, :] = state[j * rows : (j + 1) * rows, :]
        send_ref[j, rows:, :] = spread


def prefix_kernel(n_ctx, got_ref, send_ref, totals_ref):
    rows = HEAD_DIM // n_ctx
    state = jnp.zeros((rows, HEAD_DIM), f32)
    for j in range(n_ctx):
        send_ref[j] = state
        total = got_ref[j, rows:, :]
        totals_ref[j] = total
        state = jnp.exp(total) * state + got_ref[j, :rows, :]


def suffix_kernel(n_ctx, got_ref, totals_ref, send_ref):
    rows = HEAD_DIM // n_ctx
    state = jnp.zeros((rows, HEAD_DIM), f32)
    for j in reversed(range(n_ctx)):
        send_ref[j] = state
        state = jnp.exp(totals_ref[j]) * state + got_ref[j]


def local_kernel(q_ref, k_ref, v_ref, sums_ref, turned_ref, out_ref):
    length = q_ref.shape[0]
    sums, turned = sums_ref[...], turned_ref[...]
    for b in range(length // BLOCK):
        at = b * BLOCK
        for i in range(BLOCK // TILE):
            rows = slice(at + i * TILE, at + (i + 1) * TILE)
            cols = slice(at, at + (i + 1) * TILE)
            scores = dot(q_ref[rows, :], k_ref[cols, :], 1, 1)
            weights = (scores * weights_tile(sums, turned, at, i)).astype(bf16)
            out_ref[rows, :] = dot(weights, v_ref[cols, :])


def gate_kernel(gate_ref, grad_ref, gain_ref, prob_ref, signal_ref):
    prob = jax.nn.sigmoid(gate_ref[...].astype(f32))
    prob_ref[...] = prob
    signal_ref[...] = grad_ref[...].astype(f32) * prob * gain_ref[...]


def row_sums(x):
    ones = jnp.ones((8, HEAD_DIM), bf16)
    flat = exact_dot(ones, x, 1, 1)
    rows = x.shape[0] // CHUNK
    at = lax.broadcasted_iota(jnp.int32, (rows, CHUNK), 0)
    out = flat[:, :CHUNK]
    for r in range(1, rows):
        out = jnp.where(at == r, flat[:, r * CHUNK : (r + 1) * CHUNK], out)
    return out


def attn_kernel(
    n_exp, q_ref, local_ref, state_ref, entry_ref, sums_ref, turned_ref, signal_ref,
    attn_ref, entries_ref, send_ref,
):
    length = q_ref.shape[0]
    sums, turned = sums_ref[...], turned_ref[...]
    state = state_ref[...]
    for b in range(length // BLOCK):
        at = b * BLOCK
        rows = slice(at, at + BLOCK)
        if b:
            state = entry_ref[b - 1] + jnp.exp(last) * state_ref[...]
        entries_ref[b] = state
        front = jnp.exp(column(turned, at, BLOCK))
        attn_ref[rows, :] = local_ref[rows, :] + front * exact_dot(q_ref[rows, :], state)
        last = last_of(sums, b) + (last if b else 0.0)
    attn = attn_ref[...]
    squares = row_sums(attn * attn)
    dots = row_sums(signal_ref[...] * attn)
    for j in range(n_exp):
        send_ref[j, :8, :] = squares
        send_ref[j, 8:, :] = dots


def relay_kernel(n_exp, n_section, got_ref, send_ref):
    total = got_ref[0]
    for j in range(1, n_exp):
        total = total + got_ref[j]
    for j in range(n_section):
        send_ref[j] = total


def grad_kernel(
    n_section, width, n_ctx, got_ref, attn_ref, signal_ref, q_ref, sums_ref, turned_ref,
    grad_ref, send_ref, arrive_ref, inverse_ref,
):
    length = q_ref.shape[0]
    sums, turned = sums_ref[...], turned_ref[...]
    total = got_ref[0]
    for j in range(1, n_section):
        total = total + got_ref[j]
    inverse = lax.rsqrt(total[:8] / width + EPSILON)
    along = inverse * total[8:] / width
    both = jnp.concatenate([inverse, along], axis=0).T
    inverse_ref[...] = both
    state = None
    for b in reversed(range(length // BLOCK)):
        at = b * BLOCK
        rows = slice(at, at + BLOCK)
        inv = column(both[:, :8], at, BLOCK)
        alo = column(both[:, 8:], at, BLOCK)
        normed = attn_ref[rows, :] * inv
        grad = (inv * (signal_ref[rows, :] - normed * alo)).astype(bf16)
        grad_ref[rows, :] = grad
        front = jnp.exp(column(turned, at, BLOCK))
        update = exact_dot(q_ref[rows, :], grad.astype(f32) * front, 0, 0)
        if state is None:
            state = update
            if b:
                arrive_ref[b - 1] = state
        else:
            state = jnp.exp(last_of(sums, b)) * state + update
            if b:
                arrive_ref[b - 1] = state
    part = HEAD_DIM // n_ctx
    for j in range(n_ctx):
        send_ref[j] = state[j * part : (j + 1) * part, :]


def output_kernel(
    attn_ref, inverse_ref, prob_ref, gain_ref, gout_ref, layer_ref, gate_ref,
):
    length = attn_ref.shape[0]
    both = inverse_ref[...]
    for b in range(length // BLOCK):
        at = b * BLOCK
        rows = slice(at, at + BLOCK)
        scaled = attn_ref[rows, :] * column(both[:, :8], at, BLOCK) * gain_ref[...]
        prob = prob_ref[rows, :]
        layer = scaled * prob
        layer_ref[rows, :] = layer.astype(bf16)
        gate_ref[rows, :] = (gout_ref[rows, :].astype(f32) * layer * (1.0 - prob)).astype(bf16)


def backward_kernel(
    q_ref, k_ref, v_ref, grad_ref, entries_ref, arrive_ref, sums_ref, turned_ref,
    gq_ref, gk_ref, gv_ref,
):
    length = q_ref.shape[0]
    blocks = length // BLOCK
    sums, turned = sums_ref[...], turned_ref[...]
    for b in range(blocks):
        at = b * BLOCK
        whole = slice(at, at + BLOCK)
        if b < blocks - 1:
            tail = jnp.exp(last_of(sums, b) - column(turned, at, BLOCK))
            later = arrive_ref[b]
            gk_ref[whole, :] = tail * exact_dot(v_ref[whole, :], later, 1, 1)
            gv_ref[whole, :] = tail * exact_dot(k_ref[whole, :], later)
        else:
            gk_ref[whole, :] = jnp.zeros((BLOCK, HEAD_DIM), f32)
            gv_ref[whole, :] = jnp.zeros((BLOCK, HEAD_DIM), f32)
        for i in range(BLOCK // TILE):
            rows = slice(at + i * TILE, at + (i + 1) * TILE)
            cols = slice(at, at + (i + 1) * TILE)
            table = weights_tile(sums, turned, at, i)
            q, g = q_ref[rows, :], grad_ref[rows, :]
            wq = (dot(q, k_ref[cols, :], 1, 1) * table).astype(bf16)
            gw = (dot(g, v_ref[cols, :], 1, 1) * table).astype(bf16)
            front = jnp.exp(column(turned, at + i * TILE, TILE))
            grad_q = dot(gw, k_ref[cols, :]) + front * exact_dot(g, entries_ref[b], 1, 1)
            gq_ref[rows, :] = grad_q.astype(bf16)
            gk_ref[cols, :] += dot(gw, q, 0, 0)
            gv_ref[cols, :] += dot(wq, g, 0, 0)


def finish_kernel(k_ref, v_ref, gk_ref, gv_ref, state_ref, sums_ref, turned_ref, ok_ref, ov_ref):
    length = k_ref.shape[0]
    blocks = length // BLOCK
    sums, turned = sums_ref[...], turned_ref[...]
    after = jnp.zeros((1, 1), f32)
    for b in reversed(range(blocks)):
        at = b * BLOCK
        rows = slice(at, at + BLOCK)
        tail = jnp.exp(last_of(sums, b) - column(turned, at, BLOCK))
        state = state_ref[...] * jnp.exp(after) if b < blocks - 1 else state_ref[...]
        after = after + last_of(sums, b)
        ok_ref[rows, :] = (gk_ref[rows, :] + tail * exact_dot(v_ref[rows, :], state, 1, 1)).astype(bf16)
        ov_ref[rows, :] = (gv_ref[rows, :] + tail * exact_dot(k_ref[rows, :], state)).astype(bf16)


def call(kernel, name, out, *args, cost=2e6):
    shapes = [jax.ShapeDtypeStruct(s, d) for s, d in out]
    return pl.pallas_call(
        kernel,
        out_shape=shapes,
        in_specs=[pl.BlockSpec(memory_space=pltpu.VMEM)] * len(args),
        out_specs=[pl.BlockSpec(memory_space=pltpu.VMEM)] * len(out),
        compiler_params=pltpu.CompilerParams(vmem_limit_bytes=32 << 20),
        cost_estimate=pl.CostEstimate(flops=int(cost), bytes_accessed=int(cost), transcendentals=0),
        name=name,
    )(*args)


def exchange(x, axis):
    return lax.all_to_all(x, axis, 0, 0)


def on_device(queries, key_rows, value_rows, gate_input, norm_gain, log_decay, grad_output):
    length = queries.shape[0]
    n_ctx, n_exp, n_section = (lax.axis_size(a) for a in ("ctx", "exp", "section"))
    width = HEAD_DIM * n_exp * n_section
    blocks = length // BLOCK
    chunks = length // CHUNK
    part = HEAD_DIM // n_ctx
    rates = log_decay.reshape(chunks, CHUNK)
    gain = norm_gain.reshape(1, HEAD_DIM)
    full, half = ((length, HEAD_DIM), f32), ((length, HEAD_DIM), bf16)
    states = ((blocks, HEAD_DIM, HEAD_DIM), f32)
    inner = ((max(blocks - 1, 1), HEAD_DIM, HEAD_DIM), f32)

    sent, entry, sums, turned = call(
        partial(states_kernel, n_ctx), "states",
        [((n_ctx, 2 * part, HEAD_DIM), f32), inner, ((chunks, CHUNK), f32), ((CHUNK, chunks), f32)],
        key_rows, value_rows, rates,
    )
    got = exchange(sent, "ctx")
    (local,) = call(local_kernel, "local", [full], queries, key_rows, value_rows, sums, turned)
    prefix, totals = call(
        partial(prefix_kernel, n_ctx), "prefix",
        [((n_ctx, part, HEAD_DIM), f32)] * 2, got,
    )
    state = exchange(prefix, "ctx").reshape(HEAD_DIM, HEAD_DIM)
    prob, signal = call(gate_kernel, "gate", [full, full], gate_input, grad_output, gain)
    attn, entries, sent = call(
        partial(attn_kernel, n_exp), "attn", [full, states, ((n_exp, 16, CHUNK), f32)],
        queries, local, state, entry, sums, turned, signal,
    )
    got = exchange(sent, "exp")
    (sent,) = call(
        partial(relay_kernel, n_exp, n_section), "relay", [((n_section, 16, CHUNK), f32)], got
    )
    got = exchange(sent, "section")
    grad, sent, arrive, inverse = call(
        partial(grad_kernel, n_section, width, n_ctx), "grad",
        [half, ((n_ctx, part, HEAD_DIM), f32), inner, ((CHUNK, 2 * chunks), f32)],
        got, attn, signal, queries, sums, turned,
    )
    got = exchange(sent, "ctx")
    grad_q, local_k, local_v = call(
        backward_kernel, "backward", [half, full, full],
        queries, key_rows, value_rows, grad, entries, arrive, sums, turned,
    )
    (suffix,) = call(
        partial(suffix_kernel, n_ctx), "suffix", [((n_ctx, part, HEAD_DIM), f32)], got, totals
    )
    later = exchange(suffix, "ctx").reshape(HEAD_DIM, HEAD_DIM)
    layer_out, grad_gate = call(
        output_kernel, "output", [half, half], attn, inverse, prob, gain, grad_output
    )
    grad_k, grad_v = call(
        finish_kernel, "finish", [half, half],
        key_rows, value_rows, local_k, local_v, later, sums, turned,
    )
    return layer_out, grad_q, grad_k, grad_v, grad_gate


def solution(mesh):
    block = P("ctx", ("section", "exp"))
    in_specs = (
        block, block, block, block, P(("section", "exp")), P(("section", "exp"), "ctx"), block,
    )
    return jax.shard_map(
        on_device, mesh=mesh, in_specs=in_specs, out_specs=(block,) * 5, check_vma=False
    )
```

```python
from functools import partial

import jax
import jax.numpy as jnp
from jax import lax
from jax.experimental import pallas as pl
from jax.experimental.pallas import tpu as pltpu
from jax.sharding import PartitionSpec as P

HEAD_DIM = 128
BLOCK = 512
TILE = 256
CHUNK = 128
EPSILON = 1e-06
f32 = jnp.float32
bf16 = jnp.bfloat16


def dot(a, b, ca=1, cb=0):
    return lax.dot_general(a, b, (((ca,), (cb,)), ((), ())), preferred_element_type=f32)


def split3(x):
    hi = x.astype(bf16)
    rest = x - hi.astype(f32)
    mid = rest.astype(bf16)
    return hi, mid, (rest - mid.astype(f32)).astype(bf16)


def exact_dot(a, b, turned=False):
    hi, mid, lo = split3(b)
    twice = jnp.concatenate([a, a], axis=1)
    zero = jnp.zeros_like(hi)
    if turned:
        left = jnp.concatenate([hi, mid], axis=1)
        right = jnp.concatenate([lo, zero], axis=1)
        both = dot(twice, jnp.concatenate([left, right], axis=0), 1, 1)
    else:
        left = jnp.concatenate([hi, mid], axis=0)
        right = jnp.concatenate([lo, zero], axis=0)
        both = dot(twice, jnp.concatenate([left, right], axis=1))
    half = both.shape[1] // 2
    return both[:, :half] + both[:, half:]


def exact_outer(a, b):
    parts = dot(a, jnp.concatenate(split3(b), axis=1), 0, 0)
    width = b.shape[1]
    return parts[:, :width] + (parts[:, width : 2 * width] + parts[:, 2 * width :])


def cumulate(rates):
    rows = rates.shape[0]
    per_block = BLOCK // CHUNK
    r = lax.broadcasted_iota(jnp.int32, (CHUNK, CHUNK), 0)
    c = lax.broadcasted_iota(jnp.int32, (CHUNK, CHUNK), 1)
    upper = jnp.where(r <= c, 1.0, 0.0).astype(bf16)
    hi, mid, lo = split3(rates)
    within = dot(hi, upper) + (dot(mid, upper) + dot(lo, upper))
    total = within[:, CHUNK - 1 :]
    pieces = []
    for row in range(rows):
        value = within[row : row + 1, :]
        for earlier in range(row // per_block * per_block, row):
            value = value + total[earlier : earlier + 1, :]
        pieces.append(value)
    return jnp.concatenate(pieces, axis=0)


def column(turned, first, count):
    return jnp.concatenate(
        [turned[:, r : r + 1] for r in range(first // CHUNK, (first + count) // CHUNK)], axis=0
    )


def row_of(sums, first, count):
    return jnp.concatenate(
        [sums[r : r + 1, :] for r in range(first // CHUNK, (first + count) // CHUNK)], axis=1
    )


def last_of(sums, block):
    row = (block + 1) * BLOCK // CHUNK - 1
    return sums[row : row + 1, CHUNK - 1 :]


def weights_tile(sums, turned, start, tile):
    first = start + tile * TILE
    width = (tile + 1) * TILE
    gap = column(turned, first, TILE) - row_of(sums, start, width)
    lower = jnp.exp(jnp.minimum(gap, 0.0))
    t = lax.broadcasted_iota(jnp.int32, (TILE, width), 0) + tile * TILE
    s = lax.broadcasted_iota(jnp.int32, (TILE, width), 1)
    return jnp.where(t >= s, lower, 0.0)


def core_of():
    return lax.rem(lax.axis_index("ctx"), 2)


def states_kernel(
    k_hbm, v_hbm, rates_hbm, send_ref, keep_ref, entry_ref, sums_ref, turned_ref,
    k_ref, v_ref, rates_ref, state_ref, sems,
):
    length = k_ref.shape[0]
    blocks = length // BLOCK
    half = HEAD_DIM // 2
    copies = [pltpu.make_async_copy(rates_hbm, rates_ref, sems.at[0])]
    for b in range(blocks):
        rows = pl.ds(b * BLOCK, BLOCK)
        copies.append(pltpu.make_async_copy(v_hbm.at[rows], v_ref.at[rows], sems.at[2 * b + 1]))
        copies.append(pltpu.make_async_copy(k_hbm.at[rows], k_ref.at[rows], sems.at[2 * b + 2]))
    for copy in copies:
        copy.start()
    copies[0].wait()
    sums = cumulate(rates_ref[...])
    turned = sums.T
    sums_ref[...] = sums
    turned_ref[...] = turned
    state = None
    total = jnp.zeros((1, 1), f32)
    for b in range(blocks):
        at = b * BLOCK
        last = last_of(sums, b)
        tail = jnp.exp(last - column(turned, at, BLOCK))
        copies[2 * b + 1].wait()
        copies[2 * b + 2].wait()
        scaled = v_ref[at : at + BLOCK, :].astype(f32) * tail
        update = exact_outer(k_ref[at : at + BLOCK, :], scaled)
        state = update if state is None else jnp.exp(last) * state + update
        total = total + last
        if b < blocks - 1:
            entry_ref[b] = state
    state_ref[...] = state
    core = core_of()
    spread = jnp.broadcast_to(total, (8, HEAD_DIM))
    keep_ref[:half, :] = state_ref[pl.ds(pl.multiple_of(core * half, half), half), :]
    keep_ref[half:, :] = spread
    send_ref[:half, :] = state_ref[pl.ds(pl.multiple_of((1 - core) * half, half), half), :]
    send_ref[half:, :] = spread


def pair_kernel(n_chip, keep_ref, got_ref, send_ref, first_ref, totals_ref):
    half = HEAD_DIM // 2
    is_second = core_of() == 1
    mine, other = keep_ref[:half, :], got_ref[:half, :]
    mine_total, other_total = keep_ref[half:, :], got_ref[half:, :]
    first = jnp.where(is_second, other, mine)
    second = jnp.where(is_second, mine, other)
    second_total = jnp.where(is_second, mine_total, other_total)
    first_ref[...] = first
    totals_ref[:8, :] = jnp.where(is_second, other_total, mine_total)
    totals_ref[8:, :] = second_total
    chip = jnp.exp(second_total[:1, :]) * first + second
    for j in range(n_chip):
        send_ref[j, :half, :] = chip
        send_ref[j, half:, :] = mine_total + other_total


def prefix_kernel(n_chip, got_ref, first_ref, totals_ref, keep_ref, send_ref, chips_ref):
    half = HEAD_DIM // 2
    chip = lax.div(lax.axis_index("ctx"), 2)
    is_second = core_of() == 1
    state = jnp.zeros((half, HEAD_DIM), f32)
    for j in range(n_chip):
        total = got_ref[j, half : half + 1, :]
        chips_ref[j : j + 1, :] = total
        state = jnp.where(j < chip, jnp.exp(total) * state + got_ref[j, :half, :], state)
    after = jnp.exp(totals_ref[:1, :]) * state + first_ref[...]
    keep_ref[...] = jnp.where(is_second, after, state)
    send_ref[...] = jnp.where(is_second, state, after)


def back_pair_kernel(n_chip, keep_ref, got_ref, totals_ref, send_ref, second_ref):
    is_second = core_of() == 1
    mine, other = keep_ref[...], got_ref[...]
    first = jnp.where(is_second, other, mine)
    second = jnp.where(is_second, mine, other)
    second_ref[...] = second
    chip = jnp.exp(totals_ref[:1, :]) * second + first
    for j in range(n_chip):
        send_ref[j] = chip


def suffix_kernel(
    n_chip, got_ref, second_ref, totals_ref, chips_ref, after_ref, keep_ref, send_ref,
):
    del after_ref
    half = HEAD_DIM // 2
    chip = lax.div(lax.axis_index("ctx"), 2)
    is_second = core_of() == 1
    state = jnp.zeros((half, HEAD_DIM), f32)
    for j in reversed(range(n_chip)):
        total = chips_ref[j : j + 1, :]
        state = jnp.where(j > chip, jnp.exp(total) * state + got_ref[j], state)
    before = jnp.exp(totals_ref[8:9, :]) * state + second_ref[...]
    keep_ref[...] = jnp.where(is_second, state, before)
    send_ref[...] = jnp.where(is_second, before, state)


def whole_state(keep_ref, got_ref):
    is_second = core_of() == 1
    keep, got = keep_ref[...], got_ref[...]
    return jnp.concatenate(
        [jnp.where(is_second, got, keep), jnp.where(is_second, keep, got)], axis=0
    )


def local_kernel(q_ref, k_ref, v_ref, sums_ref, turned_ref, out_ref):
    length = q_ref.shape[0]
    sums, turned = sums_ref[...], turned_ref[...]
    for b in range(length // BLOCK):
        at = b * BLOCK
        for i in range(BLOCK // TILE):
            rows = slice(at + i * TILE, at + (i + 1) * TILE)
            cols = slice(at, at + (i + 1) * TILE)
            scores = dot(q_ref[rows, :], k_ref[cols, :], 1, 1)
            weights = (scores * weights_tile(sums, turned, at, i)).astype(bf16)
            out_ref[rows, :] = dot(weights, v_ref[cols, :])


def gate_kernel(gate_ref, grad_ref, gain_ref, signal_ref):
    prob = jax.nn.sigmoid(gate_ref[...].astype(f32))
    signal_ref[...] = grad_ref[...].astype(f32) * prob * gain_ref[...]


def row_sums(x):
    ones = jnp.ones((8, HEAD_DIM), bf16)
    flat = exact_dot(ones, x, True)
    rows = x.shape[0] // CHUNK
    at = lax.broadcasted_iota(jnp.int32, (rows, CHUNK), 0)
    out = flat[:, :CHUNK]
    for r in range(1, rows):
        out = jnp.where(at == r, flat[:, r * CHUNK : (r + 1) * CHUNK], out)
    return out


def attn_kernel(
    n_section, q_ref, local_ref, keep_ref, got_ref, entry_ref, sums_ref, turned_ref, signal_ref,
    attn_ref, send_ref,
):
    length = q_ref.shape[0]
    sums, turned = sums_ref[...], turned_ref[...]
    start = whole_state(keep_ref, got_ref)
    state, gone = start, jnp.zeros((1, 1), f32)
    for b in range(length // BLOCK):
        at = b * BLOCK
        rows = slice(at, at + BLOCK)
        if b:
            state = entry_ref[b - 1] + jnp.exp(gone) * start
        attn_ref[length + b * HEAD_DIM : length + (b + 1) * HEAD_DIM, :] = state
        front = jnp.exp(column(turned, at, BLOCK))
        attn_ref[rows, :] = local_ref[rows, :] + front * exact_dot(q_ref[rows, :], state)
        gone = gone + last_of(sums, b)
    attn = attn_ref[:length, :]
    squares = row_sums(attn * attn)
    dots = row_sums(signal_ref[...] * attn)
    for j in range(n_section):
        send_ref[j, :8, :] = squares
        send_ref[j, 8:, :] = dots


def relay_kernel(n_section, n_exp, got_ref, send_ref):
    total = got_ref[0]
    for j in range(1, n_section):
        total = total + got_ref[j]
    for j in range(n_exp):
        send_ref[j] = total


def grad_kernel(
    n_exp, width, got_ref, attn_ref, signal_ref, q_ref, sums_ref, turned_ref,
    grad_ref, keep_ref, send_ref, aux_ref, state_ref,
):
    length = q_ref.shape[0]
    half = HEAD_DIM // 2
    blocks = length // BLOCK
    sums, turned = sums_ref[...], turned_ref[...]
    total = got_ref[0]
    for j in range(1, n_exp):
        total = total + got_ref[j]
    inverse = lax.rsqrt(total[:8] / width + EPSILON)
    along = inverse * total[8:] / width
    both = jnp.concatenate([inverse, along], axis=0).T
    aux_ref[(blocks - 1) * HEAD_DIM :, :16] = both
    state = None
    for b in reversed(range(blocks)):
        at = b * BLOCK
        rows = slice(at, at + BLOCK)
        inv = column(both[:, :8], at, BLOCK)
        alo = column(both[:, 8:], at, BLOCK)
        normed = attn_ref[rows, :] * inv
        grad = (inv * (signal_ref[rows, :] - normed * alo)).astype(bf16)
        grad_ref[rows, :] = grad
        front = jnp.exp(column(turned, at, BLOCK))
        update = exact_outer(q_ref[rows, :], grad.astype(f32) * front)
        state = update if state is None else jnp.exp(last_of(sums, b)) * state + update
        if b:
            aux_ref[(b - 1) * HEAD_DIM : b * HEAD_DIM, :] = state
    state_ref[...] = state
    core = core_of()
    keep_ref[...] = state_ref[pl.ds(pl.multiple_of(core * half, half), half), :]
    send_ref[...] = state_ref[pl.ds(pl.multiple_of((1 - core) * half, half), half), :]


def backward_kernel(
    q_ref, k_ref, v_ref, grad_ref, attn_ref, aux_ref, sums_ref, turned_ref, gin_ref, gain_ref, gout_ref,
    layer_hbm, gate_hbm, gq_hbm, gk_ref, gv_ref, layer_ref, gate_ref, gq_ref, sems,
):
    length = q_ref.shape[0]
    blocks = length // BLOCK
    sums, turned = sums_ref[...], turned_ref[...]
    both = aux_ref[(blocks - 1) * HEAD_DIM :, :16]
    copies = []

    def leave(ref, hbm, b, kind):
        part = pl.ds(b * BLOCK, BLOCK)
        copies.append(pltpu.make_async_copy(ref.at[part], hbm.at[part], sems.at[3 * b + kind]))
        copies[-1].start()

    for b in range(blocks):
        rows = slice(b * BLOCK, (b + 1) * BLOCK)
        scaled = attn_ref[rows, :] * column(both[:, :8], b * BLOCK, BLOCK) * gain_ref[...]
        prob = jax.nn.sigmoid(gin_ref[rows, :].astype(f32))
        layer = scaled * prob
        layer_ref[rows, :] = layer.astype(bf16)
        leave(layer_ref, layer_hbm, b, 0)
        gate_ref[rows, :] = (gout_ref[rows, :].astype(f32) * layer * (1.0 - prob)).astype(bf16)
        leave(gate_ref, gate_hbm, b, 1)
    for b in range(blocks):
        at = b * BLOCK
        whole = slice(at, at + BLOCK)
        if b < blocks - 1:
            tail = jnp.exp(last_of(sums, b) - column(turned, at, BLOCK))
            later = aux_ref[b * HEAD_DIM : (b + 1) * HEAD_DIM, :]
            gk_ref[whole, :] = tail * exact_dot(v_ref[whole, :], later, True)
            gv_ref[whole, :] = tail * exact_dot(k_ref[whole, :], later)
        else:
            gk_ref[whole, :] = jnp.zeros((BLOCK, HEAD_DIM), f32)
            gv_ref[whole, :] = jnp.zeros((BLOCK, HEAD_DIM), f32)
        entering = attn_ref[length + b * HEAD_DIM : length + (b + 1) * HEAD_DIM, :]
        for i in range(BLOCK // TILE):
            rows = slice(at + i * TILE, at + (i + 1) * TILE)
            cols = slice(at, at + (i + 1) * TILE)
            table = weights_tile(sums, turned, at, i)
            q, g = q_ref[rows, :], grad_ref[rows, :]
            wq = (dot(q, k_ref[cols, :], 1, 1) * table).astype(bf16)
            gw = (dot(g, v_ref[cols, :], 1, 1) * table).astype(bf16)
            front = jnp.exp(column(turned, at + i * TILE, TILE))
            grad_q = dot(gw, k_ref[cols, :]) + front * exact_dot(g, entering, True)
            gq_ref[rows, :] = grad_q.astype(bf16)
            gk_ref[cols, :] += dot(gw, q, 0, 0)
            gv_ref[cols, :] += dot(wq, g, 0, 0)
        leave(gq_ref, gq_hbm, b, 2)
    for copy in copies:
        copy.wait()


def finish_kernel(
    k_ref, v_ref, gk_ref, gv_ref, keep_ref, got_ref, sums_ref, turned_ref, ok_hbm, ov_hbm,
    ok_ref, ov_ref, sems,
):
    length = k_ref.shape[0]
    blocks = length // BLOCK
    sums, turned = sums_ref[...], turned_ref[...]
    start = whole_state(keep_ref, got_ref)
    after = jnp.zeros((1, 1), f32)
    copies = []
    for b in reversed(range(blocks)):
        at = b * BLOCK
        rows = slice(at, at + BLOCK)
        tail = jnp.exp(last_of(sums, b) - column(turned, at, BLOCK))
        state = start * jnp.exp(after)
        after = after + last_of(sums, b)
        part = pl.ds(at, BLOCK)
        ok_ref[rows, :] = (gk_ref[rows, :] + tail * exact_dot(v_ref[rows, :], state, True)).astype(bf16)
        copies.append(pltpu.make_async_copy(ok_ref.at[part], ok_hbm.at[part], sems.at[2 * b]))
        copies[-1].start()
        ov_ref[rows, :] = (gv_ref[rows, :] + tail * exact_dot(k_ref[rows, :], state)).astype(bf16)
        copies.append(pltpu.make_async_copy(ov_ref.at[part], ov_hbm.at[part], sems.at[2 * b + 1]))
        copies[-1].start()
    for copy in copies:
        copy.wait()


def call(kernel, name, out, *args, cost=2e6, hbm_in=False, hbm_last=False, hbm_out=0, scratch=()):
    shapes = [jax.ShapeDtypeStruct(s, d) for s, d in out]
    places = [pltpu.HBM if hbm_in else pltpu.VMEM] * len(args)
    if hbm_last:
        places[-1] = pl.ANY
    place_out = [pltpu.HBM] * hbm_out + [pltpu.VMEM] * (len(out) - hbm_out)
    return pl.pallas_call(
        kernel,
        out_shape=shapes,
        in_specs=[pl.BlockSpec(memory_space=place) for place in places],
        out_specs=[pl.BlockSpec(memory_space=place) for place in place_out],
        scratch_shapes=scratch,
        compiler_params=pltpu.CompilerParams(vmem_limit_bytes=16 << 20),
        cost_estimate=pl.CostEstimate(flops=int(cost), bytes_accessed=int(cost), transcendentals=0),
        name=name,
    )(*args)


def exchange(x, axis, groups=None):
    return lax.all_to_all(x, axis, 0, 0, axis_index_groups=groups)


def on_device(queries, key_rows, value_rows, gate_input, norm_gain, log_decay, grad_output):
    length = queries.shape[0]
    n_ctx, n_exp, n_section = (lax.axis_size(a) for a in ("ctx", "exp", "section"))
    n_chip = n_ctx // 2
    width = HEAD_DIM * n_exp * n_section
    blocks = length // BLOCK
    chunks = length // CHUNK
    part = HEAD_DIM // 2
    pairs = [(i, i ^ 1) for i in range(n_ctx)]
    lines = [[2 * i + core for i in range(n_chip)] for core in range(2)]
    rates = log_decay.reshape(chunks, CHUNK)
    gain = norm_gain.reshape(1, HEAD_DIM)
    full, half = ((length, HEAD_DIM), f32), ((length, HEAD_DIM), bf16)
    piece, marked = ((part, HEAD_DIM), f32), ((part + 8, HEAD_DIM), f32)

    sent, keep, entry, sums, turned = call(
        states_kernel, "states",
        [marked, marked, ((blocks - 1, HEAD_DIM, HEAD_DIM), f32), ((chunks, CHUNK), f32),
         ((CHUNK, chunks), f32)],
        *(pltpu.with_memory_space_constraint(a, pltpu.HBM) for a in (key_rows, value_rows, rates)),
        hbm_in=True,
        scratch=[
            pltpu.VMEM((length, HEAD_DIM), bf16), pltpu.VMEM((length, HEAD_DIM), bf16),
            pltpu.VMEM((chunks, CHUNK), f32), pltpu.VMEM((HEAD_DIM, HEAD_DIM), f32),
            pltpu.SemaphoreType.DMA((2 * blocks + 1,)),
        ],
    )
    got = lax.ppermute(sent, "ctx", pairs)
    sent, first, totals = call(
        partial(pair_kernel, n_chip), "pair",
        [((n_chip, part + 8, HEAD_DIM), f32), piece, ((16, HEAD_DIM), f32)], keep, got,
    )
    got = exchange(sent, "ctx", lines)
    (local,) = call(local_kernel, "local", [full], queries, key_rows, value_rows, sums, turned)
    (signal,) = call(gate_kernel, "gate", [full], gate_input, grad_output, gain)
    keep, sent, chips = call(
        partial(prefix_kernel, n_chip), "prefix", [piece, piece, ((n_chip, HEAD_DIM), f32)],
        got, first, totals,
    )
    got = lax.ppermute(sent, "ctx", pairs)
    attn, sent = call(
        partial(attn_kernel, n_section), "attn",
        [((length + blocks * HEAD_DIM, HEAD_DIM), f32), ((n_section, 16, CHUNK), f32)],
        queries, local, keep, got, entry, sums, turned, signal,
    )
    got = exchange(sent, "section")
    (sent,) = call(
        partial(relay_kernel, n_section, n_exp), "relay", [((n_exp, 16, CHUNK), f32)], got
    )
    got = exchange(sent, "exp")
    grad, keep, sent, aux = call(
        partial(grad_kernel, n_exp, width), "grad",
        [half, piece, piece, ((blocks * HEAD_DIM, HEAD_DIM), f32)],
        got, attn, signal, queries, sums, turned,
        scratch=[pltpu.VMEM((HEAD_DIM, HEAD_DIM), f32)],
    )
    got = lax.ppermute(sent, "ctx", pairs)
    sent, second = call(
        partial(back_pair_kernel, n_chip), "back_pair",
        [((n_chip, part, HEAD_DIM), f32), piece], keep, got, totals,
    )
    got = exchange(sent, "ctx", lines)
    layer_out, grad_gate, grad_q, local_k, local_v = call(
        backward_kernel, "backward", [half, half, half, full, full],
        queries, key_rows, value_rows, grad, attn, aux, sums, turned, gate_input, gain, grad_output,
        hbm_out=3, scratch=[
            pltpu.VMEM((length, HEAD_DIM), bf16), pltpu.VMEM((length, HEAD_DIM), bf16),
            pltpu.VMEM((length, HEAD_DIM), bf16), pltpu.SemaphoreType.DMA((3 * blocks,)),
        ],
    )
    keep, sent = call(
        partial(suffix_kernel, n_chip), "suffix", [piece, piece], got, second, totals, chips, local_k, hbm_last=True,
    )
    got = lax.ppermute(sent, "ctx", pairs)
    grad_k, grad_v = call(
        finish_kernel, "finish", [half, half],
        key_rows, value_rows, local_k, local_v, keep, got, sums, turned, hbm_out=2,
        scratch=[
            pltpu.VMEM((length, HEAD_DIM), bf16), pltpu.VMEM((length, HEAD_DIM), bf16),
            pltpu.SemaphoreType.DMA((2 * blocks,)),
        ],
    )
    return layer_out, grad_q, grad_k, grad_v, grad_gate


def solution(mesh):
    block = P("ctx", ("section", "exp"))
    in_specs = (
        block, block, block, block, P(("section", "exp")), P(("section", "exp"), "ctx"), block,
    )
    return jax.shard_map(
        on_device, mesh=mesh, in_specs=in_specs, out_specs=(block,) * 5, check_vma=False
    )
```

```python
from functools import partial

import jax
import jax.numpy as jnp
from jax import lax
from jax.experimental import pallas as pl
from jax.experimental.pallas import tpu as pltpu
from jax.sharding import PartitionSpec as P

HEAD_DIM = 128
BLOCK = 512
TILE = 256
CHUNK = 128
EPSILON = 1e-06
f32 = jnp.float32
bf16 = jnp.bfloat16


def dot(a, b, ca=1, cb=0):
    return lax.dot_general(a, b, (((ca,), (cb,)), ((), ())), preferred_element_type=f32)


def split3(x):
    hi = x.astype(bf16)
    rest = x - hi.astype(f32)
    mid = rest.astype(bf16)
    return hi, mid, (rest - mid.astype(f32)).astype(bf16)


def exact_dot(a, b, turned=False):
    hi, mid, lo = split3(b)
    twice = jnp.concatenate([a, a], axis=1)
    zero = jnp.zeros_like(hi)
    if turned:
        left = jnp.concatenate([hi, mid], axis=1)
        right = jnp.concatenate([lo, zero], axis=1)
        both = dot(twice, jnp.concatenate([left, right], axis=0), 1, 1)
    else:
        left = jnp.concatenate([hi, mid], axis=0)
        right = jnp.concatenate([lo, zero], axis=0)
        both = dot(twice, jnp.concatenate([left, right], axis=1))
    half = both.shape[1] // 2
    return both[:, :half] + both[:, half:]


def exact_outer(a, b):
    parts = dot(a, jnp.concatenate(split3(b), axis=1), 0, 0)
    width = b.shape[1]
    return parts[:, :width] + (parts[:, width : 2 * width] + parts[:, 2 * width :])


def cumulate(rates):
    rows = rates.shape[0]
    per_block = BLOCK // CHUNK
    r = lax.broadcasted_iota(jnp.int32, (CHUNK, CHUNK), 0)
    c = lax.broadcasted_iota(jnp.int32, (CHUNK, CHUNK), 1)
    upper = jnp.where(r <= c, 1.0, 0.0).astype(bf16)
    hi, mid, lo = split3(rates)
    within = dot(hi, upper) + (dot(mid, upper) + dot(lo, upper))
    total = within[:, CHUNK - 1 :]
    pieces = []
    for row in range(rows):
        value = within[row : row + 1, :]
        for earlier in range(row // per_block * per_block, row):
            value = value + total[earlier : earlier + 1, :]
        pieces.append(value)
    return jnp.concatenate(pieces, axis=0)


def column(turned, first, count, kind=0):
    skip = 8 * kind
    return jnp.concatenate(
        [turned[:, skip + r : skip + r + 1] for r in range(first // CHUNK, (first + count) // CHUNK)],
        axis=0,
    )


def row_of(sums, first, count):
    return jnp.concatenate(
        [sums[r : r + 1, :] for r in range(first // CHUNK, (first + count) // CHUNK)], axis=1
    )


def last_of(sums, block):
    row = (block + 1) * BLOCK // CHUNK - 1
    return sums[row : row + 1, CHUNK - 1 :]


def weights_tile(sums, turned, start, tile):
    first = start + tile * TILE
    width = (tile + 1) * TILE
    gap = column(turned, first, TILE) - row_of(sums, start, width)
    lower = jnp.exp(jnp.minimum(gap, 0.0))
    t = lax.broadcasted_iota(jnp.int32, (TILE, width), 0) + tile * TILE
    s = lax.broadcasted_iota(jnp.int32, (TILE, width), 1)
    return jnp.where(t >= s, lower, 0.0)


def core_of():
    return lax.rem(lax.axis_index("ctx"), 2)


def states_kernel(
    k_hbm, v_hbm, rates_hbm, gain_hbm, send_ref, keep_ref, entry_ref, sums_ref, turned_ref, gain_ref, k_ref, v_ref,
    rates_ref, state_ref, sems,
):
    length = k_ref.shape[0]
    blocks = length // BLOCK
    half = HEAD_DIM // 2
    copies = [pltpu.make_async_copy(rates_hbm, rates_ref, sems.at[0])]
    for b in range(blocks):
        rows = pl.ds(b * BLOCK, BLOCK)
        copies.append(pltpu.make_async_copy(v_hbm.at[rows], v_ref.at[rows], sems.at[2 * b + 1]))
        copies.append(pltpu.make_async_copy(k_hbm.at[rows], k_ref.at[rows], sems.at[2 * b + 2]))
    copies.append(pltpu.make_async_copy(gain_hbm, gain_ref, sems.at[2 * blocks + 1]))
    for copy in copies:
        copy.start()
    copies[0].wait()
    sums = cumulate(rates_ref[...])
    row = lax.broadcasted_iota(jnp.int32, sums.shape, 0)
    lasts = last_of(sums, 0)
    for b in range(1, blocks):
        lasts = jnp.where(row >= b * BLOCK // CHUNK, last_of(sums, b), lasts)
    front = jnp.exp(sums)
    tails = jnp.exp(lasts - sums)
    turned = jnp.concatenate([sums, front, tails, jnp.zeros_like(sums)], axis=0).T
    sums_ref[...] = sums
    turned_ref[...] = turned
    state = None
    total = jnp.zeros((1, 1), f32)
    for b in range(blocks):
        at = b * BLOCK
        last = last_of(sums, b)
        tail = column(turned, at, BLOCK, 2)
        copies[2 * b + 1].wait()
        copies[2 * b + 2].wait()
        scaled = v_ref[at : at + BLOCK, :].astype(f32) * tail
        update = exact_outer(k_ref[at : at + BLOCK, :], scaled)
        state = update if state is None else jnp.exp(last) * state + update
        total = total + last
        if b < blocks - 1:
            entry_ref[b] = state
    state_ref[...] = state
    core = core_of()
    spread = jnp.broadcast_to(total, (8, HEAD_DIM))
    keep_ref[:half, :] = state_ref[pl.ds(pl.multiple_of(core * half, half), half), :]
    keep_ref[half:, :] = spread
    send_ref[:half, :] = state_ref[pl.ds(pl.multiple_of((1 - core) * half, half), half), :]
    send_ref[half:, :] = spread
    copies[-1].wait()


def pair_kernel(n_chip, keep_ref, got_ref, after_ref, send_ref, first_ref, totals_ref):
    del after_ref
    half = HEAD_DIM // 2
    is_second = core_of() == 1
    mine, other = keep_ref[:half, :], got_ref[:half, :]
    mine_total, other_total = keep_ref[half:, :], got_ref[half:, :]
    first = jnp.where(is_second, other, mine)
    second = jnp.where(is_second, mine, other)
    second_total = jnp.where(is_second, mine_total, other_total)
    first_ref[...] = first
    totals_ref[:8, :] = jnp.where(is_second, other_total, mine_total)
    totals_ref[8:, :] = second_total
    chip = jnp.exp(second_total[:1, :]) * first + second
    for j in range(n_chip):
        send_ref[j, :half, :] = chip
        send_ref[j, half:, :] = mine_total + other_total


def prefix_kernel(n_chip, got_ref, first_ref, totals_ref, keep_ref, send_ref, chips_ref):
    half = HEAD_DIM // 2
    chip = lax.div(lax.axis_index("ctx"), 2)
    is_second = core_of() == 1
    state = jnp.zeros((half, HEAD_DIM), f32)
    for j in range(n_chip):
        total = got_ref[j, half : half + 1, :]
        chips_ref[j : j + 1, :] = total
        state = jnp.where(j < chip, jnp.exp(total) * state + got_ref[j, :half, :], state)
    after = jnp.exp(totals_ref[:1, :]) * state + first_ref[...]
    keep_ref[...] = jnp.where(is_second, after, state)
    send_ref[...] = jnp.where(is_second, state, after)


def back_pair_kernel(n_chip, keep_ref, got_ref, totals_ref, after_ref, send_ref, second_ref):
    del after_ref
    is_second = core_of() == 1
    mine, other = keep_ref[...], got_ref[...]
    first = jnp.where(is_second, other, mine)
    second = jnp.where(is_second, mine, other)
    second_ref[...] = second
    chip = jnp.exp(totals_ref[:1, :]) * second + first
    for j in range(n_chip):
        send_ref[j] = chip


def suffix_kernel(n_chip, got_ref, second_ref, totals_ref, chips_ref, keep_ref, send_ref):
    half = HEAD_DIM // 2
    chip = lax.div(lax.axis_index("ctx"), 2)
    is_second = core_of() == 1
    state = jnp.zeros((half, HEAD_DIM), f32)
    for j in reversed(range(n_chip)):
        total = chips_ref[j : j + 1, :]
        state = jnp.where(j > chip, jnp.exp(total) * state + got_ref[j], state)
    before = jnp.exp(totals_ref[8:9, :]) * state + second_ref[...]
    keep_ref[...] = jnp.where(is_second, state, before)
    send_ref[...] = jnp.where(is_second, before, state)


def whole_state(keep_ref, got_ref):
    is_second = core_of() == 1
    keep, got = keep_ref[...], got_ref[...]
    return jnp.concatenate(
        [jnp.where(is_second, got, keep), jnp.where(is_second, keep, got)], axis=0
    )


def local_kernel(q_ref, k_ref, v_ref, sums_ref, turned_ref, out_ref):
    length = q_ref.shape[0]
    sums, turned = sums_ref[...], turned_ref[...]
    for b in range(length // BLOCK):
        at = b * BLOCK
        for i in range(BLOCK // TILE):
            rows = slice(at + i * TILE, at + (i + 1) * TILE)
            cols = slice(at, at + (i + 1) * TILE)
            scores = dot(q_ref[rows, :], k_ref[cols, :], 1, 1)
            weights = (scores * weights_tile(sums, turned, at, i)).astype(bf16)
            out_ref[rows, :] = dot(weights, v_ref[cols, :])


def gate_kernel(gate_ref, grad_ref, gain_ref, signal_ref):
    prob = jax.nn.sigmoid(gate_ref[...].astype(f32))
    signal_ref[...] = grad_ref[...].astype(f32) * prob * gain_ref[...]


def row_sums(x):
    down = lax.broadcasted_iota(jnp.int32, (CHUNK, CHUNK), 0)
    across = lax.broadcasted_iota(jnp.int32, (CHUNK, CHUNK), 1)
    pieces = []
    for r in range(x.shape[0] // CHUNK):
        sums = jnp.sum(x[r * CHUNK : (r + 1) * CHUNK, :], axis=1, keepdims=True)
        pieces.append(jnp.sum(jnp.where(down == across, sums, 0.0), axis=0, keepdims=True))
    return jnp.concatenate(pieces, axis=0)


def attn_kernel(
    n_section, q_ref, local_ref, keep_ref, got_ref, entry_ref, sums_ref, turned_ref, signal_ref,
    attn_ref, send_ref,
):
    length = q_ref.shape[0]
    sums, turned = sums_ref[...], turned_ref[...]
    start = whole_state(keep_ref, got_ref)
    state, gone = start, jnp.zeros((1, 1), f32)
    for b in range(length // BLOCK):
        at = b * BLOCK
        rows = slice(at, at + BLOCK)
        if b:
            state = entry_ref[b - 1] + jnp.exp(gone) * start
        attn_ref[length + b * HEAD_DIM : length + (b + 1) * HEAD_DIM, :] = state
        front = column(turned, at, BLOCK, 1)
        attn_ref[rows, :] = local_ref[rows, :] + front * exact_dot(q_ref[rows, :], state)
        gone = gone + last_of(sums, b)
    attn = attn_ref[:length, :]
    squares = row_sums(attn * attn)
    dots = row_sums(signal_ref[...] * attn)
    for j in range(n_section):
        send_ref[j, :8, :] = squares
        send_ref[j, 8:, :] = dots


def relay_kernel(n_section, n_exp, got_ref, send_ref):
    total = got_ref[0]
    for j in range(1, n_section):
        total = total + got_ref[j]
    for j in range(n_exp):
        send_ref[j] = total


def grad_kernel(
    n_exp, width, got_ref, attn_ref, signal_ref, q_ref, sums_ref, turned_ref,
    grad_ref, keep_ref, send_ref, aux_ref, state_ref,
):
    length = q_ref.shape[0]
    half = HEAD_DIM // 2
    blocks = length // BLOCK
    sums, turned = sums_ref[...], turned_ref[...]
    total = got_ref[0]
    for j in range(1, n_exp):
        total = total + got_ref[j]
    inverse = lax.rsqrt(total[:8] / width + EPSILON)
    along = inverse * total[8:] / width
    both = jnp.concatenate([inverse, inverse * inverse * along], axis=0).T
    aux_ref[(blocks - 1) * HEAD_DIM :, :16] = both
    state = None
    for b in reversed(range(blocks)):
        at = b * BLOCK
        rows = slice(at, at + BLOCK)
        inv = column(both[:, :8], at, BLOCK)
        alo = column(both[:, 8:], at, BLOCK)
        grad = (inv * signal_ref[rows, :] - alo * attn_ref[rows, :]).astype(bf16)
        grad_ref[rows, :] = grad
        front = column(turned, at, BLOCK, 1)
        update = exact_outer(q_ref[rows, :], grad.astype(f32) * front)
        state = update if state is None else jnp.exp(last_of(sums, b)) * state + update
        if b:
            aux_ref[(b - 1) * HEAD_DIM : b * HEAD_DIM, :] = state
    state_ref[...] = state
    core = core_of()
    keep_ref[...] = state_ref[pl.ds(pl.multiple_of(core * half, half), half), :]
    send_ref[...] = state_ref[pl.ds(pl.multiple_of((1 - core) * half, half), half), :]


def output_kernel(
    attn_ref, aux_ref, gin_ref, gain_ref, gout_ref, layer_hbm, gate_hbm, done_ref, layer_ref, gate_ref, sems,
):
    length = gout_ref.shape[0]
    done_ref[...] = jnp.zeros_like(done_ref)
    both = aux_ref[aux_ref.shape[0] - HEAD_DIM :, :16]
    copies = []
    for b in range(length // BLOCK):
        rows, part = slice(b * BLOCK, (b + 1) * BLOCK), pl.ds(b * BLOCK, BLOCK)
        scaled = attn_ref[rows, :] * column(both, b * BLOCK, BLOCK) * gain_ref[...]
        prob = jax.nn.sigmoid(gin_ref[rows, :].astype(f32))
        layer = scaled * prob
        layer_ref[rows, :] = layer.astype(bf16)
        copies.append(pltpu.make_async_copy(layer_ref.at[part], layer_hbm.at[part], sems.at[2 * b]))
        copies[-1].start()
        gate_ref[rows, :] = (gout_ref[rows, :].astype(f32) * layer * (1.0 - prob)).astype(bf16)
        copies.append(pltpu.make_async_copy(gate_ref.at[part], gate_hbm.at[part], sems.at[2 * b + 1]))
        copies[-1].start()
    for copy in copies:
        copy.wait()


def backward_kernel(
    q_ref, k_ref, v_ref, grad_ref, attn_ref, aux_ref, sums_ref, turned_ref,
    gq_hbm, gk_ref, gv_ref, gq_ref, sems,
):
    length = q_ref.shape[0]
    blocks = length // BLOCK
    sums, turned = sums_ref[...], turned_ref[...]
    copies = []
    for b in range(blocks):
        at = b * BLOCK
        whole = slice(at, at + BLOCK)
        later = None
        if b < blocks - 1:
            later = aux_ref[b * HEAD_DIM : (b + 1) * HEAD_DIM, :]
        entering = attn_ref[length + b * HEAD_DIM : length + (b + 1) * HEAD_DIM, :]
        for i in range(BLOCK // TILE):
            rows = slice(at + i * TILE, at + (i + 1) * TILE)
            cols = slice(at, at + (i + 1) * TILE)
            table = weights_tile(sums, turned, at, i)
            q, g = q_ref[rows, :], grad_ref[rows, :]
            wq = (dot(q, k_ref[cols, :], 1, 1) * table).astype(bf16)
            gw = (dot(g, v_ref[cols, :], 1, 1) * table).astype(bf16)
            front = column(turned, at + i * TILE, TILE, 1)
            grad_q = dot(gw, k_ref[cols, :]) + front * exact_dot(g, entering, True)
            gq_ref[rows, :] = grad_q.astype(bf16)
            add_k, add_v = dot(gw, q, 0, 0), dot(wq, g, 0, 0)
            if later is not None:
                tail = column(turned, at + i * TILE, TILE, 2)
                more_k = tail * exact_dot(v_ref[rows, :], later, True)
                more_v = tail * exact_dot(k_ref[rows, :], later)
            else:
                more_k = more_v = 0.0
            if i:
                old = slice(at, at + i * TILE)
                gk_ref[old, :] += add_k[: i * TILE, :]
                gv_ref[old, :] += add_v[: i * TILE, :]
            gk_ref[rows, :] = add_k[i * TILE :, :] + more_k
            gv_ref[rows, :] = add_v[i * TILE :, :] + more_v
        part = pl.ds(at, BLOCK)
        copies.append(pltpu.make_async_copy(gq_ref.at[part], gq_hbm.at[part], sems.at[b]))
        copies[-1].start()
    for copy in copies:
        copy.wait()


def finish_kernel(
    k_ref, v_ref, gk_ref, gv_ref, keep_ref, got_ref, sums_ref, turned_ref, ok_hbm, ov_hbm,
    ok_ref, ov_ref, sems,
):
    length = k_ref.shape[0]
    blocks = length // BLOCK
    sums, turned = sums_ref[...], turned_ref[...]
    start = whole_state(keep_ref, got_ref)
    after = jnp.zeros((1, 1), f32)
    copies = []
    for b in reversed(range(blocks)):
        at = b * BLOCK
        rows = slice(at, at + BLOCK)
        tail = column(turned, at, BLOCK, 2)
        state = start * jnp.exp(after)
        after = after + last_of(sums, b)
        part = pl.ds(at, BLOCK)
        ok_ref[rows, :] = (gk_ref[rows, :] + tail * exact_dot(v_ref[rows, :], state, True)).astype(bf16)
        copies.append(pltpu.make_async_copy(ok_ref.at[part], ok_hbm.at[part], sems.at[2 * b]))
        copies[-1].start()
        ov_ref[rows, :] = (gv_ref[rows, :] + tail * exact_dot(k_ref[rows, :], state)).astype(bf16)
        copies.append(pltpu.make_async_copy(ov_ref.at[part], ov_hbm.at[part], sems.at[2 * b + 1]))
        copies[-1].start()
    for copy in copies:
        copy.wait()


def call(kernel, name, out, *args, cost=2e6, hbm_in=False, hbm_last=False, hbm_out=0, scratch=()):
    shapes = [jax.ShapeDtypeStruct(s, d) for s, d in out]
    places = [pltpu.HBM if hbm_in else pltpu.VMEM] * len(args)
    if hbm_last:
        places[-1] = pl.ANY
    place_out = [pltpu.HBM] * hbm_out + [pltpu.VMEM] * (len(out) - hbm_out)
    return pl.pallas_call(
        kernel,
        out_shape=shapes,
        in_specs=[pl.BlockSpec(memory_space=place) for place in places],
        out_specs=[pl.BlockSpec(memory_space=place) for place in place_out],
        scratch_shapes=scratch,
        compiler_params=pltpu.CompilerParams(vmem_limit_bytes=16 << 20),
        cost_estimate=pl.CostEstimate(flops=int(cost), bytes_accessed=int(cost), transcendentals=0),
        name=name,
    )(*args)


def exchange(x, axis, groups=None):
    return lax.all_to_all(x, axis, 0, 0, axis_index_groups=groups)


def on_device(queries, key_rows, value_rows, gate_input, norm_gain, log_decay, grad_output):
    length = queries.shape[0]
    n_ctx, n_exp, n_section = (lax.axis_size(a) for a in ("ctx", "exp", "section"))
    n_chip = n_ctx // 2
    width = HEAD_DIM * n_exp * n_section
    blocks = length // BLOCK
    chunks = length // CHUNK
    part = HEAD_DIM // 2
    pairs = [(i, i ^ 1) for i in range(n_ctx)]
    lines = [[2 * i + core for i in range(n_chip)] for core in range(2)]
    rates = log_decay.reshape(chunks, CHUNK)
    full, half = ((length, HEAD_DIM), f32), ((length, HEAD_DIM), bf16)
    piece, marked = ((part, HEAD_DIM), f32), ((part + 8, HEAD_DIM), f32)

    sent, keep, entry, sums, turned, gain, held_k, held_v = call(
        states_kernel, "states",
        [marked, marked, ((blocks - 1, HEAD_DIM, HEAD_DIM), f32), ((chunks, CHUNK), f32),
         ((CHUNK, 4 * chunks), f32), ((1, HEAD_DIM), f32), half, half],
        *(
            pltpu.with_memory_space_constraint(a, pltpu.HBM)
            for a in (key_rows, value_rows, rates, norm_gain.reshape(1, HEAD_DIM))
        ),
        hbm_in=True, cost=1e7,
        scratch=[
            pltpu.VMEM((chunks, CHUNK), f32), pltpu.VMEM((HEAD_DIM, HEAD_DIM), f32),
            pltpu.SemaphoreType.DMA((2 * blocks + 2,)),
        ],
    )
    got = lax.ppermute(sent, "ctx", pairs)
    (local,) = call(local_kernel, "local", [full], queries, held_k, held_v, sums, turned)
    sent, first, totals = call(
        partial(pair_kernel, n_chip), "pair",
        [((n_chip, part + 8, HEAD_DIM), f32), piece, ((16, HEAD_DIM), f32)],
        keep, got, local, hbm_last=True,
    )
    got = exchange(sent, "ctx", lines)
    (signal,) = call(gate_kernel, "gate", [full], gate_input, grad_output, gain)
    keep, sent, chips = call(
        partial(prefix_kernel, n_chip), "prefix", [piece, piece, ((n_chip, HEAD_DIM), f32)],
        got, first, totals,
    )
    got = lax.ppermute(sent, "ctx", pairs)
    attn, sent = call(
        partial(attn_kernel, n_section), "attn",
        [((length + blocks * HEAD_DIM, HEAD_DIM), f32), ((n_section, 16, CHUNK), f32)],
        queries, local, keep, got, entry, sums, turned, signal,
    )
    got = exchange(sent, "section")
    (sent,) = call(
        partial(relay_kernel, n_section, n_exp), "relay", [((n_exp, 16, CHUNK), f32)], got
    )
    got = exchange(sent, "exp")
    grad, keep, sent, aux = call(
        partial(grad_kernel, n_exp, width), "grad",
        [half, piece, piece, ((blocks * HEAD_DIM, HEAD_DIM), f32)],
        got, attn, signal, queries, sums, turned,
        scratch=[pltpu.VMEM((HEAD_DIM, HEAD_DIM), f32)],
    )
    got = lax.ppermute(sent, "ctx", pairs)
    layer_out, grad_gate, done = call(
        output_kernel, "output", [half, half, ((8, HEAD_DIM), f32)], attn, aux, gate_input, gain, grad_output, hbm_out=2,
        scratch=[
            pltpu.VMEM((length, HEAD_DIM), bf16), pltpu.VMEM((length, HEAD_DIM), bf16),
            pltpu.SemaphoreType.DMA((2 * blocks,)),
        ],
    )
    sent, second = call(
        partial(back_pair_kernel, n_chip), "back_pair",
        [((n_chip, part, HEAD_DIM), f32), piece], keep, got, totals, done,
    )
    got = exchange(sent, "ctx", lines)
    grad_q, local_k, local_v = call(
        backward_kernel, "backward", [half, full, full],
        queries, held_k, held_v, grad, attn, aux, sums, turned, hbm_out=1,
        scratch=[pltpu.VMEM((length, HEAD_DIM), bf16), pltpu.SemaphoreType.DMA((blocks,))],
    )
    keep, sent = call(
        partial(suffix_kernel, n_chip), "suffix", [piece, piece], got, second, totals, chips
    )
    got = lax.ppermute(sent, "ctx", pairs)
    grad_k, grad_v = call(
        finish_kernel, "finish", [half, half],
        held_k, held_v, local_k, local_v, keep, got, sums, turned, hbm_out=2,
        scratch=[
            pltpu.VMEM((length, HEAD_DIM), bf16), pltpu.VMEM((length, HEAD_DIM), bf16),
            pltpu.SemaphoreType.DMA((2 * blocks,)),
        ],
    )
    return layer_out, grad_q, grad_k, grad_v, grad_gate


def solution(mesh):
    block = P("ctx", ("section", "exp"))
    in_specs = (
        block, block, block, block, P(("section", "exp")), P(("section", "exp"), "ctx"), block,
    )
    return jax.shard_map(
        on_device, mesh=mesh, in_specs=in_specs, out_specs=(block,) * 5, check_vma=False
    )
```

```python
from functools import partial

import jax
import jax.numpy as jnp
from jax import lax
from jax.experimental import pallas as pl
from jax.experimental.pallas import tpu as pltpu
from jax.sharding import PartitionSpec as P

HEAD_DIM = 128
BLOCK = 512
TILE = 256
CHUNK = 128
EPSILON = 1e-06
f32 = jnp.float32
bf16 = jnp.bfloat16


def dot(a, b, ca=1, cb=0):
    return lax.dot_general(a, b, (((ca,), (cb,)), ((), ())), preferred_element_type=f32)


def split3(x):
    hi = x.astype(bf16)
    rest = x - hi.astype(f32)
    mid = rest.astype(bf16)
    return hi, mid, (rest - mid.astype(f32)).astype(bf16)


def exact_dot(a, b, turned=False):
    hi, mid, lo = split3(b)
    twice = jnp.concatenate([a, a], axis=1)
    zero = jnp.zeros_like(hi)
    if turned:
        left = jnp.concatenate([hi, mid], axis=1)
        right = jnp.concatenate([lo, zero], axis=1)
        both = dot(twice, jnp.concatenate([left, right], axis=0), 1, 1)
    else:
        left = jnp.concatenate([hi, mid], axis=0)
        right = jnp.concatenate([lo, zero], axis=0)
        both = dot(twice, jnp.concatenate([left, right], axis=1))
    half = both.shape[1] // 2
    return both[:, :half] + both[:, half:]


def exact_outer(a, b):
    parts = dot(a, jnp.concatenate(split3(b), axis=1), 0, 0)
    width = b.shape[1]
    return parts[:, :width] + (parts[:, width : 2 * width] + parts[:, 2 * width :])


def cumulate(rates):
    rows = rates.shape[0]
    per_block = BLOCK // CHUNK
    r = lax.broadcasted_iota(jnp.int32, (CHUNK, CHUNK), 0)
    c = lax.broadcasted_iota(jnp.int32, (CHUNK, CHUNK), 1)
    upper = jnp.where(r <= c, 1.0, 0.0).astype(bf16)
    hi, mid, lo = split3(rates)
    within = dot(hi, upper) + (dot(mid, upper) + dot(lo, upper))
    total = within[:, CHUNK - 1 :]
    pieces = []
    for row in range(rows):
        value = within[row : row + 1, :]
        for earlier in range(row // per_block * per_block, row):
            value = value + total[earlier : earlier + 1, :]
        pieces.append(value)
    return jnp.concatenate(pieces, axis=0)


def column(turned, first, count, kind=0):
    skip = 8 * kind
    return jnp.concatenate(
        [turned[:, skip + r : skip + r + 1] for r in range(first // CHUNK, (first + count) // CHUNK)],
        axis=0,
    )


def row_of(sums, first, count):
    return jnp.concatenate(
        [sums[r : r + 1, :] for r in range(first // CHUNK, (first + count) // CHUNK)], axis=1
    )


def last_of(sums, block):
    row = (block + 1) * BLOCK // CHUNK - 1
    return sums[row : row + 1, CHUNK - 1 :]


def weights_tile(sums, turned, start, tile):
    first = start + tile * TILE
    width = (tile + 1) * TILE
    gap = column(turned, first, TILE) - row_of(sums, start, width)
    lower = jnp.exp(jnp.minimum(gap, 0.0))
    t = lax.broadcasted_iota(jnp.int32, (TILE, width), 0) + tile * TILE
    s = lax.broadcasted_iota(jnp.int32, (TILE, width), 1)
    return jnp.where(t >= s, lower, 0.0)


def core_of():
    return lax.rem(lax.axis_index("ctx"), 2)


def states_kernel(
    k_hbm, v_hbm, q_hbm, rates_hbm, gain_hbm, send_ref, keep_ref, entry_ref, sums_ref, turned_ref, gain_ref, k_ref, v_ref, q_ref,
    rates_ref, state_ref, sems,
):
    length = k_ref.shape[0]
    blocks = length // BLOCK
    half = HEAD_DIM // 2
    copies = [pltpu.make_async_copy(rates_hbm, rates_ref, sems.at[0])]
    for b in range(blocks):
        rows = pl.ds(b * BLOCK, BLOCK)
        copies.append(pltpu.make_async_copy(v_hbm.at[rows], v_ref.at[rows], sems.at[2 * b + 1]))
        copies.append(pltpu.make_async_copy(k_hbm.at[rows], k_ref.at[rows], sems.at[2 * b + 2]))
    copies.append(pltpu.make_async_copy(gain_hbm, gain_ref, sems.at[2 * blocks + 1]))
    copies.append(pltpu.make_async_copy(q_hbm, q_ref, sems.at[2 * blocks + 2]))
    for copy in copies:
        copy.start()
    copies[0].wait()
    sums = cumulate(rates_ref[...])
    row = lax.broadcasted_iota(jnp.int32, sums.shape, 0)
    lasts = last_of(sums, 0)
    for b in range(1, blocks):
        lasts = jnp.where(row >= b * BLOCK // CHUNK, last_of(sums, b), lasts)
    front = jnp.exp(sums)
    tails = jnp.exp(lasts - sums)
    turned = jnp.concatenate([sums, front, tails, jnp.zeros_like(sums)], axis=0).T
    sums_ref[...] = sums
    turned_ref[...] = turned
    state = None
    total = jnp.zeros((1, 1), f32)
    for b in range(blocks):
        at = b * BLOCK
        last = last_of(sums, b)
        tail = column(turned, at, BLOCK, 2)
        copies[2 * b + 1].wait()
        copies[2 * b + 2].wait()
        scaled = v_ref[at : at + BLOCK, :].astype(f32) * tail
        update = exact_outer(k_ref[at : at + BLOCK, :], scaled)
        state = update if state is None else jnp.exp(last) * state + update
        total = total + last
        if b < blocks - 1:
            entry_ref[b] = state
    state_ref[...] = state
    core = core_of()
    spread = jnp.broadcast_to(total, (8, HEAD_DIM))
    keep_ref[:half, :] = state_ref[pl.ds(pl.multiple_of(core * half, half), half), :]
    keep_ref[half:, :] = spread
    send_ref[:half, :] = state_ref[pl.ds(pl.multiple_of((1 - core) * half, half), half), :]
    send_ref[half:, :] = spread
    copies[-2].wait()
    copies[-1].wait()


def pair_kernel(n_chip, keep_ref, got_ref, after_ref, send_ref, first_ref, totals_ref):
    del after_ref
    half = HEAD_DIM // 2
    is_second = core_of() == 1
    mine, other = keep_ref[:half, :], got_ref[:half, :]
    mine_total, other_total = keep_ref[half:, :], got_ref[half:, :]
    first = jnp.where(is_second, other, mine)
    second = jnp.where(is_second, mine, other)
    second_total = jnp.where(is_second, mine_total, other_total)
    first_ref[...] = first
    totals_ref[:8, :] = jnp.where(is_second, other_total, mine_total)
    totals_ref[8:, :] = second_total
    chip = jnp.exp(second_total[:1, :]) * first + second
    for j in range(n_chip):
        send_ref[j, :half, :] = chip
        send_ref[j, half:, :] = mine_total + other_total


def prefix_kernel(n_chip, got_ref, first_ref, totals_ref, keep_ref, send_ref, chips_ref):
    half = HEAD_DIM // 2
    chip = lax.div(lax.axis_index("ctx"), 2)
    is_second = core_of() == 1
    state = jnp.zeros((half, HEAD_DIM), f32)
    for j in range(n_chip):
        total = got_ref[j, half : half + 1, :]
        chips_ref[j : j + 1, :] = total
        state = jnp.where(j < chip, jnp.exp(total) * state + got_ref[j, :half, :], state)
    after = jnp.exp(totals_ref[:1, :]) * state + first_ref[...]
    keep_ref[...] = jnp.where(is_second, after, state)
    send_ref[...] = jnp.where(is_second, state, after)


def back_pair_kernel(n_chip, keep_ref, got_ref, totals_ref, after_ref, send_ref, second_ref):
    del after_ref
    is_second = core_of() == 1
    mine, other = keep_ref[...], got_ref[...]
    first = jnp.where(is_second, other, mine)
    second = jnp.where(is_second, mine, other)
    second_ref[...] = second
    chip = jnp.exp(totals_ref[:1, :]) * second + first
    for j in range(n_chip):
        send_ref[j] = chip


def suffix_kernel(n_chip, got_ref, second_ref, totals_ref, chips_ref, keep_ref, send_ref):
    half = HEAD_DIM // 2
    chip = lax.div(lax.axis_index("ctx"), 2)
    is_second = core_of() == 1
    state = jnp.zeros((half, HEAD_DIM), f32)
    for j in reversed(range(n_chip)):
        total = chips_ref[j : j + 1, :]
        state = jnp.where(j > chip, jnp.exp(total) * state + got_ref[j], state)
    before = jnp.exp(totals_ref[8:9, :]) * state + second_ref[...]
    keep_ref[...] = jnp.where(is_second, state, before)
    send_ref[...] = jnp.where(is_second, before, state)


def whole_state(keep_ref, got_ref):
    is_second = core_of() == 1
    keep, got = keep_ref[...], got_ref[...]
    return jnp.concatenate(
        [jnp.where(is_second, got, keep), jnp.where(is_second, keep, got)], axis=0
    )


def local_kernel(q_ref, k_ref, v_ref, sums_ref, turned_ref, out_ref, table_ref, weights_ref):
    length = q_ref.shape[0]
    sums, turned = sums_ref[...], turned_ref[...]
    for b in range(length // BLOCK):
        at = b * BLOCK
        for i in range(BLOCK // TILE):
            rows = slice(at + i * TILE, at + (i + 1) * TILE)
            cols = slice(at, at + (i + 1) * TILE)
            scores = dot(q_ref[rows, :], k_ref[cols, :], 1, 1)
            table = weights_tile(sums, turned, at, i)
            weights = (scores * table).astype(bf16)
            table_ref[rows, : (i + 1) * TILE] = table
            weights_ref[rows, : (i + 1) * TILE] = weights
            out_ref[rows, :] = dot(weights, v_ref[cols, :])


def gate_kernel(gate_ref, grad_ref, gain_ref, q_ref, sums_ref, signal_ref, fronted_ref):
    front = jnp.exp(sums_ref[...])
    for r in range(q_ref.shape[0] // CHUNK):
        at = slice(r * CHUNK, (r + 1) * CHUNK)
        parts = split3(q_ref[at, :].astype(f32).T * front[r : r + 1, :])
        for n, piece in enumerate(parts):
            fronted_ref[n * HEAD_DIM : (n + 1) * HEAD_DIM, at] = piece
    prob = jax.nn.sigmoid(gate_ref[...].astype(f32))
    signal_ref[...] = grad_ref[...].astype(f32) * prob * gain_ref[...]


def row_sums(x):
    down = lax.broadcasted_iota(jnp.int32, (CHUNK, CHUNK), 0)
    across = lax.broadcasted_iota(jnp.int32, (CHUNK, CHUNK), 1)
    pieces = []
    for r in range(x.shape[0] // CHUNK):
        sums = jnp.sum(x[r * CHUNK : (r + 1) * CHUNK, :], axis=1, keepdims=True)
        pieces.append(jnp.sum(jnp.where(down == across, sums, 0.0), axis=0, keepdims=True))
    return jnp.concatenate(pieces, axis=0)


def attn_kernel(
    n_section, q_ref, local_ref, keep_ref, got_ref, entry_ref, sums_ref, turned_ref, signal_ref,
    attn_ref, send_ref,
):
    length = q_ref.shape[0]
    sums, turned = sums_ref[...], turned_ref[...]
    start = whole_state(keep_ref, got_ref)
    state, gone = start, jnp.zeros((1, 1), f32)
    for b in range(length // BLOCK):
        at = b * BLOCK
        rows = slice(at, at + BLOCK)
        if b:
            state = entry_ref[b - 1] + jnp.exp(gone) * start
        attn_ref[length + b * HEAD_DIM : length + (b + 1) * HEAD_DIM, :] = state
        front = column(turned, at, BLOCK, 1)
        attn_ref[rows, :] = local_ref[rows, :] + front * exact_dot(q_ref[rows, :], state)
        gone = gone + last_of(sums, b)
    attn = attn_ref[:length, :]
    squares = row_sums(attn * attn)
    dots = row_sums(signal_ref[...] * attn)
    for j in range(n_section):
        send_ref[j, :8, :] = squares
        send_ref[j, 8:, :] = dots


def relay_kernel(n_section, n_exp, got_ref, send_ref):
    total = got_ref[0]
    for j in range(1, n_section):
        total = total + got_ref[j]
    for j in range(n_exp):
        send_ref[j] = total


def grad_kernel(
    n_exp, width, got_ref, attn_ref, signal_ref, fronted_ref, sums_ref,
    grad_ref, keep_ref, send_ref, aux_ref, state_ref,
):
    length = signal_ref.shape[0]
    half = HEAD_DIM // 2
    blocks = length // BLOCK
    sums = sums_ref[...]
    total = got_ref[0]
    for j in range(1, n_exp):
        total = total + got_ref[j]
    inverse = lax.rsqrt(total[:8] / width + EPSILON)
    along = inverse * total[8:] / width
    both = jnp.concatenate([inverse, inverse * inverse * along], axis=0).T
    aux_ref[(blocks - 1) * HEAD_DIM :, :16] = both
    state = None
    for b in reversed(range(blocks)):
        at = b * BLOCK
        rows = slice(at, at + BLOCK)
        inv = column(both[:, :8], at, BLOCK)
        alo = column(both[:, 8:], at, BLOCK)
        grad = (inv * signal_ref[rows, :] - alo * attn_ref[rows, :]).astype(bf16)
        grad_ref[rows, :] = grad
        parts = dot(fronted_ref[:, rows], grad)
        update = parts[:HEAD_DIM] + (parts[HEAD_DIM : 2 * HEAD_DIM] + parts[2 * HEAD_DIM :])
        state = update if state is None else jnp.exp(last_of(sums, b)) * state + update
        if b:
            aux_ref[(b - 1) * HEAD_DIM : b * HEAD_DIM, :] = state
    state_ref[...] = state
    core = core_of()
    keep_ref[...] = state_ref[pl.ds(pl.multiple_of(core * half, half), half), :]
    send_ref[...] = state_ref[pl.ds(pl.multiple_of((1 - core) * half, half), half), :]


def output_kernel(
    attn_ref, aux_ref, gin_ref, gain_ref, gout_ref, k_ref, v_ref, turned_ref,
    layer_hbm, gate_hbm, base_k_ref, base_v_ref, layer_ref, gate_ref, sems,
):
    length = gout_ref.shape[0]
    both = aux_ref[aux_ref.shape[0] - HEAD_DIM :, :16]
    copies = []
    for b in range(length // BLOCK):
        rows, part = slice(b * BLOCK, (b + 1) * BLOCK), pl.ds(b * BLOCK, BLOCK)
        scaled = attn_ref[rows, :] * column(both, b * BLOCK, BLOCK) * gain_ref[...]
        prob = jax.nn.sigmoid(gin_ref[rows, :].astype(f32))
        layer = scaled * prob
        layer_ref[rows, :] = layer.astype(bf16)
        copies.append(pltpu.make_async_copy(layer_ref.at[part], layer_hbm.at[part], sems.at[2 * b]))
        copies[-1].start()
        gate_ref[rows, :] = (gout_ref[rows, :].astype(f32) * layer * (1.0 - prob)).astype(bf16)
        copies.append(pltpu.make_async_copy(gate_ref.at[part], gate_hbm.at[part], sems.at[2 * b + 1]))
        copies[-1].start()
    turned = turned_ref[...]
    for b in range(length // BLOCK - 1):
        rows = slice(b * BLOCK, (b + 1) * BLOCK)
        tail = column(turned, b * BLOCK, BLOCK, 2)
        later = aux_ref[b * HEAD_DIM : (b + 1) * HEAD_DIM, :]
        base_k_ref[rows, :] = tail * exact_dot(v_ref[rows, :], later, True)
        base_v_ref[rows, :] = tail * exact_dot(k_ref[rows, :], later)
    for copy in copies:
        copy.wait()


def backward_kernel(
    q_ref, k_ref, v_ref, grad_ref, attn_ref, base_k_ref, base_v_ref, table_ref, weights_ref, turned_ref,
    gq_hbm, gk_ref, gv_ref, gq_ref, sems,
):
    length = q_ref.shape[0]
    blocks = length // BLOCK
    turned = turned_ref[...]
    copies = []
    for b in range(blocks):
        at = b * BLOCK
        entering = attn_ref[length + b * HEAD_DIM : length + (b + 1) * HEAD_DIM, :]
        for i in range(BLOCK // TILE):
            rows = slice(at + i * TILE, at + (i + 1) * TILE)
            cols = slice(at, at + (i + 1) * TILE)
            q, g = q_ref[rows, :], grad_ref[rows, :]
            wq = weights_ref[rows, : (i + 1) * TILE]
            table = table_ref[rows, : (i + 1) * TILE]
            gw = (dot(g, v_ref[cols, :], 1, 1) * table).astype(bf16)
            front = column(turned, at + i * TILE, TILE, 1)
            grad_q = dot(gw, k_ref[cols, :]) + front * exact_dot(g, entering, True)
            gq_ref[rows, :] = grad_q.astype(bf16)
            add_k, add_v = dot(gw, q, 0, 0), dot(wq, g, 0, 0)
            more_k = base_k_ref[rows, :] if b < blocks - 1 else 0.0
            more_v = base_v_ref[rows, :] if b < blocks - 1 else 0.0
            if i:
                old = slice(at, at + i * TILE)
                gk_ref[old, :] += add_k[: i * TILE, :]
                gv_ref[old, :] += add_v[: i * TILE, :]
            gk_ref[rows, :] = add_k[i * TILE :, :] + more_k
            gv_ref[rows, :] = add_v[i * TILE :, :] + more_v
        part = pl.ds(at, BLOCK)
        copies.append(pltpu.make_async_copy(gq_ref.at[part], gq_hbm.at[part], sems.at[b]))
        copies[-1].start()
    for copy in copies:
        copy.wait()


def finish_kernel(
    k_ref, v_ref, gk_ref, gv_ref, keep_ref, got_ref, sums_ref, turned_ref, ok_hbm, ov_hbm,
    ok_ref, ov_ref, sems,
):
    length = k_ref.shape[0]
    blocks = length // BLOCK
    sums, turned = sums_ref[...], turned_ref[...]
    start = whole_state(keep_ref, got_ref)
    after = jnp.zeros((1, 1), f32)
    copies = []
    for b in reversed(range(blocks)):
        at = b * BLOCK
        rows = slice(at, at + BLOCK)
        tail = column(turned, at, BLOCK, 2)
        state = start * jnp.exp(after)
        after = after + last_of(sums, b)
        part = pl.ds(at, BLOCK)
        ok_ref[rows, :] = (gk_ref[rows, :] + tail * exact_dot(v_ref[rows, :], state, True)).astype(bf16)
        copies.append(pltpu.make_async_copy(ok_ref.at[part], ok_hbm.at[part], sems.at[2 * b]))
        copies[-1].start()
        ov_ref[rows, :] = (gv_ref[rows, :] + tail * exact_dot(k_ref[rows, :], state)).astype(bf16)
        copies.append(pltpu.make_async_copy(ov_ref.at[part], ov_hbm.at[part], sems.at[2 * b + 1]))
        copies[-1].start()
    for copy in copies:
        copy.wait()


def call(kernel, name, out, *args, cost=2e6, hbm_in=False, hbm_last=False, hbm_out=0, scratch=()):
    shapes = [jax.ShapeDtypeStruct(s, d) for s, d in out]
    places = [pltpu.HBM if hbm_in else pltpu.VMEM] * len(args)
    if hbm_last:
        places[-1] = pl.ANY
    place_out = [pltpu.HBM] * hbm_out + [pltpu.VMEM] * (len(out) - hbm_out)
    return pl.pallas_call(
        kernel,
        out_shape=shapes,
        in_specs=[pl.BlockSpec(memory_space=place) for place in places],
        out_specs=[pl.BlockSpec(memory_space=place) for place in place_out],
        scratch_shapes=scratch,
        compiler_params=pltpu.CompilerParams(vmem_limit_bytes=16 << 20),
        cost_estimate=pl.CostEstimate(flops=int(cost), bytes_accessed=int(cost), transcendentals=0),
        name=name,
    )(*args)


def exchange(x, axis, groups=None):
    return lax.all_to_all(x, axis, 0, 0, axis_index_groups=groups)


def on_device(queries, key_rows, value_rows, gate_input, norm_gain, log_decay, grad_output):
    length = queries.shape[0]
    n_ctx, n_exp, n_section = (lax.axis_size(a) for a in ("ctx", "exp", "section"))
    n_chip = n_ctx // 2
    width = HEAD_DIM * n_exp * n_section
    blocks = length // BLOCK
    chunks = length // CHUNK
    part = HEAD_DIM // 2
    pairs = [(i, i ^ 1) for i in range(n_ctx)]
    lines = [[2 * i + core for i in range(n_chip)] for core in range(2)]
    rates = log_decay.reshape(chunks, CHUNK)
    full, half = ((length, HEAD_DIM), f32), ((length, HEAD_DIM), bf16)
    piece, marked = ((part, HEAD_DIM), f32), ((part + 8, HEAD_DIM), f32)

    sent, keep, entry, sums, turned, gain, held_k, held_v, held_q = call(
        states_kernel, "states",
        [marked, marked, ((blocks - 1, HEAD_DIM, HEAD_DIM), f32), ((chunks, CHUNK), f32),
         ((CHUNK, 4 * chunks), f32), ((1, HEAD_DIM), f32), half, half, half],
        *(
            pltpu.with_memory_space_constraint(a, pltpu.HBM)
            for a in (key_rows, value_rows, queries, rates, norm_gain.reshape(1, HEAD_DIM))
        ),
        hbm_in=True, cost=1e7,
        scratch=[
            pltpu.VMEM((chunks, CHUNK), f32), pltpu.VMEM((HEAD_DIM, HEAD_DIM), f32),
            pltpu.SemaphoreType.DMA((2 * blocks + 3,)),
        ],
    )
    got = lax.ppermute(sent, "ctx", pairs)
    local, table, weights = call(
        local_kernel, "local", [full, ((length, BLOCK), f32), ((length, BLOCK), bf16)],
        held_q, held_k, held_v, sums, turned,
    )
    sent, first, totals = call(
        partial(pair_kernel, n_chip), "pair",
        [((n_chip, part + 8, HEAD_DIM), f32), piece, ((16, HEAD_DIM), f32)],
        keep, got, local, hbm_last=True,
    )
    got = exchange(sent, "ctx", lines)
    signal, fronted = call(
        gate_kernel, "gate", [full, ((3 * HEAD_DIM, length), bf16)],
        gate_input, grad_output, gain, held_q, sums,
    )
    keep, sent, chips = call(
        partial(prefix_kernel, n_chip), "prefix", [piece, piece, ((n_chip, HEAD_DIM), f32)],
        got, first, totals,
    )
    got = lax.ppermute(sent, "ctx", pairs)
    attn, sent = call(
        partial(attn_kernel, n_section), "attn",
        [((length + blocks * HEAD_DIM, HEAD_DIM), f32), ((n_section, 16, CHUNK), f32)],
        held_q, local, keep, got, entry, sums, turned, signal,
    )
    got = exchange(sent, "section")
    (sent,) = call(
        partial(relay_kernel, n_section, n_exp), "relay", [((n_exp, 16, CHUNK), f32)], got
    )
    got = exchange(sent, "exp")
    grad, keep, sent, aux = call(
        partial(grad_kernel, n_exp, width), "grad",
        [half, piece, piece, ((blocks * HEAD_DIM, HEAD_DIM), f32)],
        got, attn, signal, fronted, sums,
        scratch=[pltpu.VMEM((HEAD_DIM, HEAD_DIM), f32)],
    )
    got = lax.ppermute(sent, "ctx", pairs)
    early = ((length - BLOCK, HEAD_DIM), f32)
    layer_out, grad_gate, base_k, base_v = call(
        output_kernel, "output", [half, half, early, early],
        attn, aux, gate_input, gain, grad_output, held_k, held_v, turned, hbm_out=2,
        scratch=[
            pltpu.VMEM((length, HEAD_DIM), bf16), pltpu.VMEM((length, HEAD_DIM), bf16),
            pltpu.SemaphoreType.DMA((2 * blocks,)),
        ],
    )
    sent, second = call(
        partial(back_pair_kernel, n_chip), "back_pair",
        [((n_chip, part, HEAD_DIM), f32), piece], keep, got, totals, base_v, hbm_last=True,
    )
    got = exchange(sent, "ctx", lines)
    grad_q, local_k, local_v = call(
        backward_kernel, "backward", [half, full, full],
        held_q, held_k, held_v, grad, attn, base_k, base_v, table, weights, turned, hbm_out=1,
        scratch=[pltpu.VMEM((length, HEAD_DIM), bf16), pltpu.SemaphoreType.DMA((blocks,))],
    )
    keep, sent = call(
        partial(suffix_kernel, n_chip), "suffix", [piece, piece], got, second, totals, chips
    )
    got = lax.ppermute(sent, "ctx", pairs)
    grad_k, grad_v = call(
        finish_kernel, "finish", [half, half],
        held_k, held_v, local_k, local_v, keep, got, sums, turned, hbm_out=2,
        scratch=[
            pltpu.VMEM((length, HEAD_DIM), bf16), pltpu.VMEM((length, HEAD_DIM), bf16),
            pltpu.SemaphoreType.DMA((2 * blocks,)),
        ],
    )
    return layer_out, grad_q, grad_k, grad_v, grad_gate


def solution(mesh):
    block = P("ctx", ("section", "exp"))
    in_specs = (
        block, block, block, block, P(("section", "exp")), P(("section", "exp"), "ctx"), block,
    )
    return jax.shard_map(
        on_device, mesh=mesh, in_specs=in_specs, out_specs=(block,) * 5, check_vma=False
    )
```

```python
from functools import partial

import jax
import jax.numpy as jnp
from jax import lax
from jax.experimental import pallas as pl
from jax.experimental.pallas import tpu as pltpu
from jax.sharding import PartitionSpec as P

HEAD_DIM = 128
BLOCK = 512
TILE = 256
CHUNK = 128
EPSILON = 1e-06
f32 = jnp.float32
bf16 = jnp.bfloat16


def dot(a, b, ca=1, cb=0):
    return lax.dot_general(a, b, (((ca,), (cb,)), ((), ())), preferred_element_type=f32)


def split3(x):
    hi = x.astype(bf16)
    rest = x - hi.astype(f32)
    mid = rest.astype(bf16)
    return hi, mid, (rest - mid.astype(f32)).astype(bf16)


def exact_dot(a, b, turned=False):
    hi, mid, lo = split3(b)
    twice = jnp.concatenate([a, a], axis=1)
    zero = jnp.zeros_like(hi)
    if turned:
        left = jnp.concatenate([hi, mid], axis=1)
        right = jnp.concatenate([lo, zero], axis=1)
        both = dot(twice, jnp.concatenate([left, right], axis=0), 1, 1)
    else:
        left = jnp.concatenate([hi, mid], axis=0)
        right = jnp.concatenate([lo, zero], axis=0)
        both = dot(twice, jnp.concatenate([left, right], axis=1))
    half = both.shape[1] // 2
    return both[:, :half] + both[:, half:]


def exact_outer(a, b):
    parts = dot(a, jnp.concatenate(split3(b), axis=1), 0, 0)
    width = b.shape[1]
    return parts[:, :width] + (parts[:, width : 2 * width] + parts[:, 2 * width :])


def cumulate(rates):
    rows = rates.shape[0]
    per_block = BLOCK // CHUNK
    r = lax.broadcasted_iota(jnp.int32, (CHUNK, CHUNK), 0)
    c = lax.broadcasted_iota(jnp.int32, (CHUNK, CHUNK), 1)
    upper = jnp.where(r <= c, 1.0, 0.0).astype(bf16)
    hi, mid, lo = split3(rates)
    within = dot(hi, upper) + (dot(mid, upper) + dot(lo, upper))
    total = within[:, CHUNK - 1 :]
    pieces = []
    for row in range(rows):
        value = within[row : row + 1, :]
        for earlier in range(row // per_block * per_block, row):
            value = value + total[earlier : earlier + 1, :]
        pieces.append(value)
    return jnp.concatenate(pieces, axis=0)


def column(turned, first, count, kind=0):
    skip = 8 * kind
    return jnp.concatenate(
        [turned[:, skip + r : skip + r + 1] for r in range(first // CHUNK, (first + count) // CHUNK)],
        axis=0,
    )


def row_of(sums, first, count):
    return jnp.concatenate(
        [sums[r : r + 1, :] for r in range(first // CHUNK, (first + count) // CHUNK)], axis=1
    )


def last_of(sums, block):
    row = (block + 1) * BLOCK // CHUNK - 1
    return sums[row : row + 1, CHUNK - 1 :]


def weights_tile(sums, turned, start, tile):
    first = start + tile * TILE
    width = (tile + 1) * TILE
    gap = column(turned, first, TILE) - row_of(sums, start, width)
    lower = jnp.exp(jnp.minimum(gap, 0.0))
    t = lax.broadcasted_iota(jnp.int32, (TILE, width), 0) + tile * TILE
    s = lax.broadcasted_iota(jnp.int32, (TILE, width), 1)
    return jnp.where(t >= s, lower, 0.0)


def core_of():
    return lax.rem(lax.axis_index("ctx"), 2)


def states_kernel(
    k_hbm, v_hbm, q_hbm, rates_hbm, gain_hbm, send_ref, keep_ref, entry_ref, sums_ref, turned_ref, gain_ref, k_ref, v_ref, q_ref,
    rates_ref, state_ref, sems,
):
    length = k_ref.shape[0]
    blocks = length // BLOCK
    half = HEAD_DIM // 2
    copies = [pltpu.make_async_copy(rates_hbm, rates_ref, sems.at[0])]
    for b in range(blocks):
        rows = pl.ds(b * BLOCK, BLOCK)
        copies.append(pltpu.make_async_copy(v_hbm.at[rows], v_ref.at[rows], sems.at[2 * b + 1]))
        copies.append(pltpu.make_async_copy(k_hbm.at[rows], k_ref.at[rows], sems.at[2 * b + 2]))
    copies.append(pltpu.make_async_copy(gain_hbm, gain_ref, sems.at[2 * blocks + 1]))
    copies.append(pltpu.make_async_copy(q_hbm, q_ref, sems.at[2 * blocks + 2]))
    for copy in copies:
        copy.start()
    copies[0].wait()
    sums = cumulate(rates_ref[...])
    row = lax.broadcasted_iota(jnp.int32, sums.shape, 0)
    lasts = last_of(sums, 0)
    for b in range(1, blocks):
        lasts = jnp.where(row >= b * BLOCK // CHUNK, last_of(sums, b), lasts)
    front = jnp.exp(sums)
    tails = jnp.exp(lasts - sums)
    turned = jnp.concatenate([sums, front, tails, jnp.zeros_like(sums)], axis=0).T
    sums_ref[...] = sums
    turned_ref[...] = turned
    state = None
    total = jnp.zeros((1, 1), f32)
    for b in range(blocks):
        at = b * BLOCK
        last = last_of(sums, b)
        tail = column(turned, at, BLOCK, 2)
        copies[2 * b + 1].wait()
        copies[2 * b + 2].wait()
        scaled = v_ref[at : at + BLOCK, :].astype(f32) * tail
        update = exact_outer(k_ref[at : at + BLOCK, :], scaled)
        state = update if state is None else jnp.exp(last) * state + update
        total = total + last
        if b < blocks - 1:
            entry_ref[b] = state
    state_ref[...] = state
    core = core_of()
    spread = jnp.broadcast_to(total, (8, HEAD_DIM))
    keep_ref[:half, :] = state_ref[pl.ds(pl.multiple_of(core * half, half), half), :]
    keep_ref[half:, :] = spread
    send_ref[:half, :] = state_ref[pl.ds(pl.multiple_of((1 - core) * half, half), half), :]
    send_ref[half:, :] = spread
    copies[-2].wait()
    copies[-1].wait()


def pair_kernel(n_chip, keep_ref, got_ref, after_ref, send_ref, first_ref, totals_ref):
    del after_ref
    half = HEAD_DIM // 2
    is_second = core_of() == 1
    mine, other = keep_ref[:half, :], got_ref[:half, :]
    mine_total, other_total = keep_ref[half:, :], got_ref[half:, :]
    first = jnp.where(is_second, other, mine)
    second = jnp.where(is_second, mine, other)
    second_total = jnp.where(is_second, mine_total, other_total)
    first_ref[...] = first
    totals_ref[:8, :] = jnp.where(is_second, other_total, mine_total)
    totals_ref[8:, :] = second_total
    chip = jnp.exp(second_total[:1, :]) * first + second
    for j in range(n_chip):
        send_ref[j, :half, :] = chip
        send_ref[j, half:, :] = mine_total + other_total


def prefix_kernel(n_chip, got_ref, first_ref, totals_ref, keep_ref, send_ref, chips_ref):
    half = HEAD_DIM // 2
    chip = lax.div(lax.axis_index("ctx"), 2)
    is_second = core_of() == 1
    state = jnp.zeros((half, HEAD_DIM), f32)
    for j in range(n_chip):
        total = got_ref[j, half : half + 1, :]
        chips_ref[j : j + 1, :] = total
        state = jnp.where(j < chip, jnp.exp(total) * state + got_ref[j, :half, :], state)
    after = jnp.exp(totals_ref[:1, :]) * state + first_ref[...]
    keep_ref[...] = jnp.where(is_second, after, state)
    send_ref[...] = jnp.where(is_second, state, after)


def back_pair_kernel(n_chip, keep_ref, got_ref, totals_ref, after_ref, send_ref, second_ref):
    del after_ref
    is_second = core_of() == 1
    mine, other = keep_ref[...], got_ref[...]
    first = jnp.where(is_second, other, mine)
    second = jnp.where(is_second, mine, other)
    second_ref[...] = second
    chip = jnp.exp(totals_ref[:1, :]) * second + first
    for j in range(n_chip):
        send_ref[j] = chip


def suffix_kernel(n_chip, got_ref, second_ref, totals_ref, chips_ref, keep_ref, send_ref):
    half = HEAD_DIM // 2
    chip = lax.div(lax.axis_index("ctx"), 2)
    is_second = core_of() == 1
    state = jnp.zeros((half, HEAD_DIM), f32)
    for j in reversed(range(n_chip)):
        total = chips_ref[j : j + 1, :]
        state = jnp.where(j > chip, jnp.exp(total) * state + got_ref[j], state)
    before = jnp.exp(totals_ref[8:9, :]) * state + second_ref[...]
    keep_ref[...] = jnp.where(is_second, state, before)
    send_ref[...] = jnp.where(is_second, before, state)


def whole_state(keep_ref, got_ref):
    is_second = core_of() == 1
    keep, got = keep_ref[...], got_ref[...]
    return jnp.concatenate(
        [jnp.where(is_second, got, keep), jnp.where(is_second, keep, got)], axis=0
    )


def local_kernel(q_ref, k_ref, v_ref, sums_ref, turned_ref, out_ref, table_ref, weights_ref):
    length = q_ref.shape[0]
    sums, turned = sums_ref[...], turned_ref[...]
    for b in range(length // BLOCK):
        at = b * BLOCK
        for i in range(BLOCK // TILE):
            rows = slice(at + i * TILE, at + (i + 1) * TILE)
            cols = slice(at, at + (i + 1) * TILE)
            scores = dot(q_ref[rows, :], k_ref[cols, :], 1, 1)
            table = weights_tile(sums, turned, at, i)
            weights = (scores * table).astype(bf16)
            table_ref[rows, : (i + 1) * TILE] = table
            weights_ref[rows, : (i + 1) * TILE] = weights
            out_ref[rows, :] = dot(weights, v_ref[cols, :])


def gate_kernel(
    gate_ref, grad_ref, gain_ref, q_ref, sums_ref, turned_ref, signal_ref, fronted_ref, front_ref,
):
    front = jnp.exp(sums_ref[...])
    for r in range(q_ref.shape[0] // CHUNK):
        at = slice(r * CHUNK, (r + 1) * CHUNK)
        front_ref[at, :] = jnp.broadcast_to(column(turned_ref[...], r * CHUNK, CHUNK, 1), (CHUNK, CHUNK))
        parts = split3(q_ref[at, :].astype(f32).T * front[r : r + 1, :])
        for n, piece in enumerate(parts):
            fronted_ref[n * HEAD_DIM : (n + 1) * HEAD_DIM, at] = piece
    prob = jax.nn.sigmoid(gate_ref[...].astype(f32))
    signal_ref[...] = grad_ref[...].astype(f32) * prob * gain_ref[...]


def row_sums(x):
    return jnp.concatenate(
        [
            jnp.sum(x[r * CHUNK : (r + 1) * CHUNK, :].T, axis=0, keepdims=True)
            for r in range(x.shape[0] // CHUNK)
        ],
        axis=0,
    )


def attn_kernel(
    n_section, q_ref, local_ref, keep_ref, got_ref, entry_ref, sums_ref, front_ref, signal_ref,
    attn_ref, send_ref,
):
    length = q_ref.shape[0]
    sums = sums_ref[...]
    start = whole_state(keep_ref, got_ref)
    state, gone = start, jnp.zeros((1, 1), f32)
    for b in range(length // BLOCK):
        at = b * BLOCK
        rows = slice(at, at + BLOCK)
        if b:
            state = entry_ref[b - 1] + jnp.exp(gone) * start
        attn_ref[length + b * HEAD_DIM : length + (b + 1) * HEAD_DIM, :] = state
        attn_ref[rows, :] = local_ref[rows, :] + front_ref[rows, :] * exact_dot(q_ref[rows, :], state)
        gone = gone + last_of(sums, b)
    attn = attn_ref[:length, :]
    squares = row_sums(attn * attn)
    dots = row_sums(signal_ref[...] * attn)
    for j in range(n_section):
        send_ref[j, :8, :] = squares
        send_ref[j, 8:, :] = dots


def relay_kernel(n_section, n_exp, got_ref, send_ref):
    total = got_ref[0]
    for j in range(1, n_section):
        total = total + got_ref[j]
    for j in range(n_exp):
        send_ref[j] = total


def grad_kernel(
    n_exp, width, got_ref, attn_ref, signal_ref, fronted_ref, sums_ref,
    grad_ref, keep_ref, send_ref, aux_ref, state_ref,
):
    length = signal_ref.shape[0]
    half = HEAD_DIM // 2
    blocks = length // BLOCK
    sums = sums_ref[...]
    total = got_ref[0]
    for j in range(1, n_exp):
        total = total + got_ref[j]
    inverse = lax.rsqrt(total[:8] / width + EPSILON)
    along = inverse * total[8:] / width
    both = jnp.concatenate([inverse, inverse * inverse * along], axis=0).T
    aux_ref[(blocks - 1) * HEAD_DIM :, :16] = both
    state = None
    for b in reversed(range(blocks)):
        at = b * BLOCK
        rows = slice(at, at + BLOCK)
        inv = column(both[:, :8], at, BLOCK)
        alo = column(both[:, 8:], at, BLOCK)
        grad = (inv * signal_ref[rows, :] - alo * attn_ref[rows, :]).astype(bf16)
        grad_ref[rows, :] = grad
        parts = dot(fronted_ref[:, rows], grad)
        update = parts[:HEAD_DIM] + (parts[HEAD_DIM : 2 * HEAD_DIM] + parts[2 * HEAD_DIM :])
        state = update if state is None else jnp.exp(last_of(sums, b)) * state + update
        if b:
            aux_ref[(b - 1) * HEAD_DIM : b * HEAD_DIM, :] = state
    state_ref[...] = state
    core = core_of()
    keep_ref[...] = state_ref[pl.ds(pl.multiple_of(core * half, half), half), :]
    send_ref[...] = state_ref[pl.ds(pl.multiple_of((1 - core) * half, half), half), :]


def output_kernel(
    attn_ref, aux_ref, gin_ref, gain_ref, gout_ref, k_ref, v_ref, turned_ref,
    layer_ref, gate_ref, base_k_ref, base_v_ref,
):
    length = gout_ref.shape[0]
    both = aux_ref[aux_ref.shape[0] - HEAD_DIM :, :16]
    for b in range(length // BLOCK):
        rows = slice(b * BLOCK, (b + 1) * BLOCK)
        scaled = attn_ref[rows, :] * column(both, b * BLOCK, BLOCK) * gain_ref[...]
        prob = jax.nn.sigmoid(gin_ref[rows, :].astype(f32))
        layer = scaled * prob
        layer_ref[rows, :] = layer.astype(bf16)
        gate_ref[rows, :] = (gout_ref[rows, :].astype(f32) * layer * (1.0 - prob)).astype(bf16)
    turned = turned_ref[...]
    for b in range(length // BLOCK - 1):
        rows = slice(b * BLOCK, (b + 1) * BLOCK)
        tail = column(turned, b * BLOCK, BLOCK, 2)
        later = aux_ref[b * HEAD_DIM : (b + 1) * HEAD_DIM, :]
        base_k_ref[rows, :] = tail * exact_dot(v_ref[rows, :], later, True)
        base_v_ref[rows, :] = tail * exact_dot(k_ref[rows, :], later)


def backward_kernel(
    q_ref, k_ref, v_ref, grad_ref, attn_ref, base_k_ref, base_v_ref, table_ref, weights_ref, front_ref,
    layer_ref, gate_ref, layer_hbm, gate_hbm, gq_ref, gk_ref, gv_ref, sems,
):
    length = q_ref.shape[0]
    blocks = length // BLOCK
    copies = [
        pltpu.make_async_copy(layer_ref, layer_hbm, sems.at[0]),
        pltpu.make_async_copy(gate_ref, gate_hbm, sems.at[1]),
    ]
    for copy in copies:
        copy.start()
    for b in range(blocks):
        at = b * BLOCK
        entering = attn_ref[length + b * HEAD_DIM : length + (b + 1) * HEAD_DIM, :]
        for i in range(BLOCK // TILE):
            rows = slice(at + i * TILE, at + (i + 1) * TILE)
            cols = slice(at, at + (i + 1) * TILE)
            q, g = q_ref[rows, :], grad_ref[rows, :]
            wq = weights_ref[rows, : (i + 1) * TILE]
            table = table_ref[rows, : (i + 1) * TILE]
            gw = (dot(g, v_ref[cols, :], 1, 1) * table).astype(bf16)
            grad_q = dot(gw, k_ref[cols, :]) + front_ref[rows, :] * exact_dot(g, entering, True)
            gq_ref[rows, :] = grad_q.astype(bf16)
            add_k, add_v = dot(gw, q, 0, 0), dot(wq, g, 0, 0)
            more_k = base_k_ref[rows, :] if b < blocks - 1 else 0.0
            more_v = base_v_ref[rows, :] if b < blocks - 1 else 0.0
            if i:
                old = slice(at, at + i * TILE)
                gk_ref[old, :] += add_k[: i * TILE, :]
                gv_ref[old, :] += add_v[: i * TILE, :]
            gk_ref[rows, :] = add_k[i * TILE :, :] + more_k
            gv_ref[rows, :] = add_v[i * TILE :, :] + more_v
    for copy in copies:
        copy.wait()


def finish_kernel(
    k_ref, v_ref, gk_ref, gv_ref, keep_ref, got_ref, sums_ref, turned_ref, gq_ref,
    ok_hbm, ov_hbm, oq_hbm, ok_ref, ov_ref, sems,
):
    length = k_ref.shape[0]
    blocks = length // BLOCK
    sums, turned = sums_ref[...], turned_ref[...]
    start = whole_state(keep_ref, got_ref)
    after = jnp.zeros((1, 1), f32)
    copies = [pltpu.make_async_copy(gq_ref, oq_hbm, sems.at[2 * blocks])]
    copies[0].start()
    for b in reversed(range(blocks)):
        at = b * BLOCK
        rows = slice(at, at + BLOCK)
        tail = column(turned, at, BLOCK, 2)
        state = start * jnp.exp(after)
        after = after + last_of(sums, b)
        part = pl.ds(at, BLOCK)
        ok_ref[rows, :] = (gk_ref[rows, :] + tail * exact_dot(v_ref[rows, :], state, True)).astype(bf16)
        copies.append(pltpu.make_async_copy(ok_ref.at[part], ok_hbm.at[part], sems.at[2 * b]))
        copies[-1].start()
        ov_ref[rows, :] = (gv_ref[rows, :] + tail * exact_dot(k_ref[rows, :], state)).astype(bf16)
        copies.append(pltpu.make_async_copy(ov_ref.at[part], ov_hbm.at[part], sems.at[2 * b + 1]))
        copies[-1].start()
    for copy in copies:
        copy.wait()


def call(kernel, name, out, *args, cost=2e6, hbm_in=False, hbm_last=False, hbm_out=0, scratch=()):
    shapes = [jax.ShapeDtypeStruct(s, d) for s, d in out]
    places = [pltpu.HBM if hbm_in else pltpu.VMEM] * len(args)
    if hbm_last:
        places[-1] = pl.ANY
    place_out = [pltpu.HBM] * hbm_out + [pltpu.VMEM] * (len(out) - hbm_out)
    return pl.pallas_call(
        kernel,
        out_shape=shapes,
        in_specs=[pl.BlockSpec(memory_space=place) for place in places],
        out_specs=[pl.BlockSpec(memory_space=place) for place in place_out],
        scratch_shapes=scratch,
        compiler_params=pltpu.CompilerParams(vmem_limit_bytes=16 << 20),
        cost_estimate=pl.CostEstimate(flops=int(cost), bytes_accessed=int(cost), transcendentals=0),
        name=name,
    )(*args)


def exchange(x, axis, groups=None):
    return lax.all_to_all(x, axis, 0, 0, axis_index_groups=groups)


def on_device(queries, key_rows, value_rows, gate_input, norm_gain, log_decay, grad_output):
    length = queries.shape[0]
    n_ctx, n_exp, n_section = (lax.axis_size(a) for a in ("ctx", "exp", "section"))
    n_chip = n_ctx // 2
    width = HEAD_DIM * n_exp * n_section
    blocks = length // BLOCK
    chunks = length // CHUNK
    part = HEAD_DIM // 2
    pairs = [(i, i ^ 1) for i in range(n_ctx)]
    lines = [[2 * i + core for i in range(n_chip)] for core in range(2)]
    rates = log_decay.reshape(chunks, CHUNK)
    full, half = ((length, HEAD_DIM), f32), ((length, HEAD_DIM), bf16)
    piece, marked = ((part, HEAD_DIM), f32), ((part + 8, HEAD_DIM), f32)

    sent, keep, entry, sums, turned, gain, held_k, held_v, held_q = call(
        states_kernel, "states",
        [marked, marked, ((blocks - 1, HEAD_DIM, HEAD_DIM), f32), ((chunks, CHUNK), f32),
         ((CHUNK, 4 * chunks), f32), ((1, HEAD_DIM), f32), half, half, half],
        *(
            pltpu.with_memory_space_constraint(a, pltpu.HBM)
            for a in (key_rows, value_rows, queries, rates, norm_gain.reshape(1, HEAD_DIM))
        ),
        hbm_in=True, cost=1e7,
        scratch=[
            pltpu.VMEM((chunks, CHUNK), f32), pltpu.VMEM((HEAD_DIM, HEAD_DIM), f32),
            pltpu.SemaphoreType.DMA((2 * blocks + 3,)),
        ],
    )
    got = lax.ppermute(sent, "ctx", pairs)
    local, table, weights = call(
        local_kernel, "local", [full, ((length, BLOCK), f32), ((length, BLOCK), bf16)],
        held_q, held_k, held_v, sums, turned,
    )
    sent, first, totals = call(
        partial(pair_kernel, n_chip), "pair",
        [((n_chip, part + 8, HEAD_DIM), f32), piece, ((16, HEAD_DIM), f32)],
        keep, got, local, hbm_last=True,
    )
    got = exchange(sent, "ctx", lines)
    signal, fronted, front = call(
        gate_kernel, "gate", [full, ((3 * HEAD_DIM, length), bf16), full],
        gate_input, grad_output, gain, held_q, sums, turned,
    )
    keep, sent, chips = call(
        partial(prefix_kernel, n_chip), "prefix", [piece, piece, ((n_chip, HEAD_DIM), f32)],
        got, first, totals,
    )
    got = lax.ppermute(sent, "ctx", pairs)
    attn, sent = call(
        partial(attn_kernel, n_section), "attn",
        [((length + blocks * HEAD_DIM, HEAD_DIM), f32), ((n_section, 16, CHUNK), f32)],
        held_q, local, keep, got, entry, sums, front, signal,
    )
    got = exchange(sent, "section")
    (sent,) = call(
        partial(relay_kernel, n_section, n_exp), "relay", [((n_exp, 16, CHUNK), f32)], got
    )
    got = exchange(sent, "exp")
    grad, keep, sent, aux = call(
        partial(grad_kernel, n_exp, width), "grad",
        [half, piece, piece, ((blocks * HEAD_DIM, HEAD_DIM), f32)],
        got, attn, signal, fronted, sums,
        scratch=[pltpu.VMEM((HEAD_DIM, HEAD_DIM), f32)],
    )
    got = lax.ppermute(sent, "ctx", pairs)
    early = ((length - BLOCK, HEAD_DIM), f32)
    layer_out, grad_gate, base_k, base_v = call(
        output_kernel, "output", [half, half, early, early],
        attn, aux, gate_input, gain, grad_output, held_k, held_v, turned,
    )
    sent, second = call(
        partial(back_pair_kernel, n_chip), "back_pair",
        [((n_chip, part, HEAD_DIM), f32), piece], keep, got, totals, base_v, hbm_last=True,
    )
    got = exchange(sent, "ctx", lines)
    layer_out, grad_gate, grad_q, local_k, local_v = call(
        backward_kernel, "backward", [half, half, half, full, full],
        held_q, held_k, held_v, grad, attn, base_k, base_v, table, weights, front,
        layer_out, grad_gate, hbm_out=2, scratch=[pltpu.SemaphoreType.DMA((2,))],
    )
    keep, sent = call(
        partial(suffix_kernel, n_chip), "suffix", [piece, piece], got, second, totals, chips
    )
    got = lax.ppermute(sent, "ctx", pairs)
    grad_k, grad_v, grad_q = call(
        finish_kernel, "finish", [half, half, half],
        held_k, held_v, local_k, local_v, keep, got, sums, turned, grad_q, hbm_out=3,
        scratch=[
            pltpu.VMEM((length, HEAD_DIM), bf16), pltpu.VMEM((length, HEAD_DIM), bf16),
            pltpu.SemaphoreType.DMA((2 * blocks + 1,)),
        ],
    )
    return layer_out, grad_q, grad_k, grad_v, grad_gate


def solution(mesh):
    block = P("ctx", ("section", "exp"))
    in_specs = (
        block, block, block, block, P(("section", "exp")), P(("section", "exp"), "ctx"), block,
    )
    return jax.shard_map(
        on_device, mesh=mesh, in_specs=in_specs, out_specs=(block,) * 5, check_vma=False
    )
```

```python
from functools import partial

import jax
import jax.numpy as jnp
from jax import lax
from jax.experimental import pallas as pl
from jax.experimental.pallas import tpu as pltpu
from jax.sharding import PartitionSpec as P

HEAD_DIM = 128
BLOCK = 512
TILE = 256
CHUNK = 128
EPSILON = 1e-06
f32 = jnp.float32
bf16 = jnp.bfloat16


def dot(a, b, ca=1, cb=0):
    return lax.dot_general(a, b, (((ca,), (cb,)), ((), ())), preferred_element_type=f32)


def split3(x):
    hi = x.astype(bf16)
    rest = x - hi.astype(f32)
    mid = rest.astype(bf16)
    return hi, mid, (rest - mid.astype(f32)).astype(bf16)


def exact_dot(a, b, turned=False):
    hi, mid, lo = split3(b)
    twice = jnp.concatenate([a, a], axis=1)
    zero = jnp.zeros_like(hi)
    if turned:
        left = jnp.concatenate([hi, mid], axis=1)
        right = jnp.concatenate([lo, zero], axis=1)
        both = dot(twice, jnp.concatenate([left, right], axis=0), 1, 1)
    else:
        left = jnp.concatenate([hi, mid], axis=0)
        right = jnp.concatenate([lo, zero], axis=0)
        both = dot(twice, jnp.concatenate([left, right], axis=1))
    half = both.shape[1] // 2
    return both[:, :half] + both[:, half:]


def exact_outer(a, b):
    parts = dot(a, jnp.concatenate(split3(b), axis=1), 0, 0)
    width = b.shape[1]
    return parts[:, :width] + (parts[:, width : 2 * width] + parts[:, 2 * width :])


def cumulate(rates):
    rows = rates.shape[0]
    per_block = BLOCK // CHUNK
    r = lax.broadcasted_iota(jnp.int32, (CHUNK, CHUNK), 0)
    c = lax.broadcasted_iota(jnp.int32, (CHUNK, CHUNK), 1)
    upper = jnp.where(r <= c, 1.0, 0.0).astype(bf16)
    hi, mid, lo = split3(rates)
    within = dot(hi, upper) + (dot(mid, upper) + dot(lo, upper))
    total = within[:, CHUNK - 1 :]
    pieces = []
    for row in range(rows):
        value = within[row : row + 1, :]
        for earlier in range(row // per_block * per_block, row):
            value = value + total[earlier : earlier + 1, :]
        pieces.append(value)
    return jnp.concatenate(pieces, axis=0)


def column(turned, first, count, kind=0):
    skip = 8 * kind
    return jnp.concatenate(
        [turned[:, skip + r : skip + r + 1] for r in range(first // CHUNK, (first + count) // CHUNK)],
        axis=0,
    )


def row_of(sums, first, count):
    return jnp.concatenate(
        [sums[r : r + 1, :] for r in range(first // CHUNK, (first + count) // CHUNK)], axis=1
    )


def last_of(sums, block):
    row = (block + 1) * BLOCK // CHUNK - 1
    return sums[row : row + 1, CHUNK - 1 :]


def weights_tile(sums, turned, start, tile):
    first = start + tile * TILE
    width = (tile + 1) * TILE
    gap = column(turned, first, TILE) - row_of(sums, start, width)
    lower = jnp.exp(jnp.minimum(gap, 0.0))
    t = lax.broadcasted_iota(jnp.int32, (TILE, width), 0) + tile * TILE
    s = lax.broadcasted_iota(jnp.int32, (TILE, width), 1)
    return jnp.where(t >= s, lower, 0.0)


def core_of():
    return lax.rem(lax.axis_index("ctx"), 2)


def states_kernel(
    k_hbm, v_hbm, q_hbm, rates_hbm, gain_hbm, send_ref, keep_ref, entry_ref, sums_ref, turned_ref, gain_ref, k_ref, v_ref, q_ref,
    rates_ref, state_ref, sems,
):
    length = k_ref.shape[0]
    blocks = length // BLOCK
    half = HEAD_DIM // 2
    copies = [pltpu.make_async_copy(rates_hbm, rates_ref, sems.at[0])]
    for b in range(blocks):
        rows = pl.ds(b * BLOCK, BLOCK)
        copies.append(pltpu.make_async_copy(v_hbm.at[rows], v_ref.at[rows], sems.at[2 * b + 1]))
        copies.append(pltpu.make_async_copy(k_hbm.at[rows], k_ref.at[rows], sems.at[2 * b + 2]))
    copies.append(pltpu.make_async_copy(gain_hbm, gain_ref, sems.at[2 * blocks + 1]))
    copies.append(pltpu.make_async_copy(q_hbm, q_ref, sems.at[2 * blocks + 2]))
    for copy in copies:
        copy.start()
    copies[0].wait()
    sums = cumulate(rates_ref[...])
    row = lax.broadcasted_iota(jnp.int32, sums.shape, 0)
    lasts = last_of(sums, 0)
    for b in range(1, blocks):
        lasts = jnp.where(row >= b * BLOCK // CHUNK, last_of(sums, b), lasts)
    front = jnp.exp(sums)
    tails = jnp.exp(lasts - sums)
    turned = jnp.concatenate([sums, front, tails, jnp.zeros_like(sums)], axis=0).T
    sums_ref[...] = sums
    turned_ref[...] = turned
    state = None
    total = jnp.zeros((1, 1), f32)
    for b in range(blocks):
        at = b * BLOCK
        last = last_of(sums, b)
        tail = column(turned, at, BLOCK, 2)
        copies[2 * b + 1].wait()
        copies[2 * b + 2].wait()
        scaled = v_ref[at : at + BLOCK, :].astype(f32) * tail
        update = exact_outer(k_ref[at : at + BLOCK, :], scaled)
        state = update if state is None else jnp.exp(last) * state + update
        total = total + last
        if b < blocks - 1:
            entry_ref[b] = state
    state_ref[...] = state
    core = core_of()
    spread = jnp.broadcast_to(total, (8, HEAD_DIM))
    keep_ref[:half, :] = state_ref[pl.ds(pl.multiple_of(core * half, half), half), :]
    keep_ref[half:, :] = spread
    send_ref[:half, :] = state_ref[pl.ds(pl.multiple_of((1 - core) * half, half), half), :]
    send_ref[half:, :] = spread
    copies[-2].wait()
    copies[-1].wait()


def pair_kernel(n_chip, keep_ref, got_ref, after_ref, send_ref, first_ref, totals_ref):
    del after_ref
    half = HEAD_DIM // 2
    is_second = core_of() == 1
    mine, other = keep_ref[:half, :], got_ref[:half, :]
    mine_total, other_total = keep_ref[half:, :], got_ref[half:, :]
    first = jnp.where(is_second, other, mine)
    second = jnp.where(is_second, mine, other)
    second_total = jnp.where(is_second, mine_total, other_total)
    first_ref[...] = first
    totals_ref[:8, :] = jnp.where(is_second, other_total, mine_total)
    totals_ref[8:, :] = second_total
    chip = jnp.exp(second_total[:1, :]) * first + second
    for j in range(n_chip):
        send_ref[j, :half, :] = chip
        send_ref[j, half:, :] = mine_total + other_total


def prefix_kernel(n_chip, got_ref, first_ref, totals_ref, keep_ref, send_ref, chips_ref):
    half = HEAD_DIM // 2
    chip = lax.div(lax.axis_index("ctx"), 2)
    is_second = core_of() == 1
    state = jnp.zeros((half, HEAD_DIM), f32)
    for j in range(n_chip):
        total = got_ref[j, half : half + 1, :]
        chips_ref[j : j + 1, :] = total
        state = jnp.where(j < chip, jnp.exp(total) * state + got_ref[j, :half, :], state)
    after = jnp.exp(totals_ref[:1, :]) * state + first_ref[...]
    keep_ref[...] = jnp.where(is_second, after, state)
    send_ref[...] = jnp.where(is_second, state, after)


def back_pair_kernel(n_chip, keep_ref, got_ref, totals_ref, after_ref, send_ref, second_ref):
    del after_ref
    is_second = core_of() == 1
    mine, other = keep_ref[...], got_ref[...]
    first = jnp.where(is_second, other, mine)
    second = jnp.where(is_second, mine, other)
    second_ref[...] = second
    chip = jnp.exp(totals_ref[:1, :]) * second + first
    for j in range(n_chip):
        send_ref[j] = chip


def suffix_kernel(n_chip, got_ref, second_ref, totals_ref, chips_ref, keep_ref, send_ref):
    half = HEAD_DIM // 2
    chip = lax.div(lax.axis_index("ctx"), 2)
    is_second = core_of() == 1
    state = jnp.zeros((half, HEAD_DIM), f32)
    for j in reversed(range(n_chip)):
        total = chips_ref[j : j + 1, :]
        state = jnp.where(j > chip, jnp.exp(total) * state + got_ref[j], state)
    before = jnp.exp(totals_ref[8:9, :]) * state + second_ref[...]
    keep_ref[...] = jnp.where(is_second, state, before)
    send_ref[...] = jnp.where(is_second, before, state)


def whole_state(keep_ref, got_ref):
    is_second = core_of() == 1
    keep, got = keep_ref[...], got_ref[...]
    return jnp.concatenate(
        [jnp.where(is_second, got, keep), jnp.where(is_second, keep, got)], axis=0
    )


def local_kernel(q_ref, k_ref, v_ref, sums_ref, turned_ref, out_ref, table_ref, weights_ref):
    length = q_ref.shape[0]
    sums, turned = sums_ref[...], turned_ref[...]
    for b in range(length // BLOCK):
        at = b * BLOCK
        for i in range(BLOCK // TILE):
            rows = slice(at + i * TILE, at + (i + 1) * TILE)
            cols = slice(at, at + (i + 1) * TILE)
            scores = dot(q_ref[rows, :], k_ref[cols, :], 1, 1)
            table = weights_tile(sums, turned, at, i)
            weights = (scores * table).astype(bf16)
            table_ref[rows, : (i + 1) * TILE] = table
            weights_ref[rows, : (i + 1) * TILE] = weights
            out_ref[rows, :] = dot(weights, v_ref[cols, :])


def gate_kernel(
    gate_ref, grad_ref, gain_ref, q_ref, sums_ref, turned_ref, signal_ref, fronted_ref, front_ref,
):
    front = jnp.exp(sums_ref[...])
    for r in range(q_ref.shape[0] // CHUNK):
        at = slice(r * CHUNK, (r + 1) * CHUNK)
        front_ref[at, :] = jnp.broadcast_to(column(turned_ref[...], r * CHUNK, CHUNK, 1), (CHUNK, CHUNK))
        parts = split3(q_ref[at, :].astype(f32).T * front[r : r + 1, :])
        for n, piece in enumerate(parts):
            fronted_ref[n * HEAD_DIM : (n + 1) * HEAD_DIM, at] = piece
    prob = jax.nn.sigmoid(gate_ref[...].astype(f32))
    signal_ref[...] = grad_ref[...].astype(f32) * prob * gain_ref[...]


def row_sums(x):
    return jnp.concatenate(
        [
            jnp.sum(x[r * CHUNK : (r + 1) * CHUNK, :].T, axis=0, keepdims=True)
            for r in range(x.shape[0] // CHUNK)
        ],
        axis=0,
    )


def attn_kernel(
    n_section, q_ref, local_ref, keep_ref, got_ref, entry_ref, sums_ref, front_ref, signal_ref,
    attn_ref, send_ref,
):
    length = q_ref.shape[0]
    sums = sums_ref[...]
    start = whole_state(keep_ref, got_ref)
    state, gone = start, jnp.zeros((1, 1), f32)
    for b in range(length // BLOCK):
        at = b * BLOCK
        rows = slice(at, at + BLOCK)
        if b:
            state = entry_ref[b - 1] + jnp.exp(gone) * start
        attn_ref[length + b * HEAD_DIM : length + (b + 1) * HEAD_DIM, :] = state
        attn_ref[rows, :] = local_ref[rows, :] + front_ref[rows, :] * exact_dot(q_ref[rows, :], state)
        gone = gone + last_of(sums, b)
    attn = attn_ref[:length, :]
    squares = row_sums(attn * attn)
    dots = row_sums(signal_ref[...] * attn)
    for j in range(n_section):
        send_ref[j, :8, :] = squares
        send_ref[j, 8:, :] = dots


def relay_kernel(n_section, n_exp, got_ref, send_ref):
    total = got_ref[0]
    for j in range(1, n_section):
        total = total + got_ref[j]
    for j in range(n_exp):
        send_ref[j] = total


def grad_kernel(
    n_exp, width, got_ref, attn_ref, signal_ref, fronted_ref, sums_ref,
    grad_ref, keep_ref, send_ref, aux_ref, state_ref,
):
    length = signal_ref.shape[0]
    half = HEAD_DIM // 2
    blocks = length // BLOCK
    sums = sums_ref[...]
    total = got_ref[0]
    for j in range(1, n_exp):
        total = total + got_ref[j]
    inverse = lax.rsqrt(total[:8] / width + EPSILON)
    along = inverse * total[8:] / width
    both = jnp.concatenate([inverse, inverse * inverse * along], axis=0).T
    aux_ref[(blocks - 1) * HEAD_DIM :, :16] = both
    state = None
    for b in reversed(range(blocks)):
        at = b * BLOCK
        rows = slice(at, at + BLOCK)
        inv = column(both[:, :8], at, BLOCK)
        alo = column(both[:, 8:], at, BLOCK)
        grad = (inv * signal_ref[rows, :] - alo * attn_ref[rows, :]).astype(bf16)
        grad_ref[rows, :] = grad
        parts = dot(fronted_ref[:, rows], grad)
        update = parts[:HEAD_DIM] + (parts[HEAD_DIM : 2 * HEAD_DIM] + parts[2 * HEAD_DIM :])
        state = update if state is None else jnp.exp(last_of(sums, b)) * state + update
        if b:
            aux_ref[(b - 1) * HEAD_DIM : b * HEAD_DIM, :] = state
    state_ref[...] = state
    core = core_of()
    keep_ref[...] = state_ref[pl.ds(pl.multiple_of(core * half, half), half), :]
    send_ref[...] = state_ref[pl.ds(pl.multiple_of((1 - core) * half, half), half), :]


def output_kernel(
    attn_ref, aux_ref, gin_ref, gain_ref, gout_ref, k_ref, v_ref, turned_ref,
    weights_ref, grad_ref, layer_ref, gate_ref, base_k_ref, gv_ref, tail_ref,
):
    length = gout_ref.shape[0]
    both = aux_ref[aux_ref.shape[0] - HEAD_DIM :, :16]
    for b in range(length // BLOCK):
        rows = slice(b * BLOCK, (b + 1) * BLOCK)
        scaled = attn_ref[rows, :] * column(both, b * BLOCK, BLOCK) * gain_ref[...]
        prob = jax.nn.sigmoid(gin_ref[rows, :].astype(f32))
        layer = scaled * prob
        layer_ref[rows, :] = layer.astype(bf16)
        gate_ref[rows, :] = (gout_ref[rows, :].astype(f32) * layer * (1.0 - prob)).astype(bf16)
    turned = turned_ref[...]
    blocks = length // BLOCK
    for b in range(blocks):
        at = b * BLOCK
        later = aux_ref[b * HEAD_DIM : (b + 1) * HEAD_DIM, :]
        for i in range(BLOCK // TILE):
            first = at + i * TILE
            rows = slice(first, first + TILE)
            tail = jnp.broadcast_to(column(turned, first, TILE, 2), (TILE, HEAD_DIM))
            tail_ref[rows, :] = tail
            add_v = dot(weights_ref[rows, : (i + 1) * TILE], grad_ref[rows, :], 0, 0)
            more_v = 0.0
            if b < blocks - 1:
                base_k_ref[rows, :] = tail * exact_dot(v_ref[rows, :], later, True)
                more_v = tail * exact_dot(k_ref[rows, :], later)
            if i:
                gv_ref[at:first, :] += add_v[: i * TILE, :]
            gv_ref[rows, :] = add_v[i * TILE :, :] + more_v


def backward_kernel(
    q_ref, k_ref, v_ref, grad_ref, attn_ref, base_k_ref, table_ref, front_ref,
    layer_ref, gate_ref, layer_hbm, gate_hbm, gq_ref, gk_ref, sems,
):
    length = q_ref.shape[0]
    blocks = length // BLOCK
    copies = [
        pltpu.make_async_copy(layer_ref, layer_hbm, sems.at[0]),
        pltpu.make_async_copy(gate_ref, gate_hbm, sems.at[1]),
    ]
    for copy in copies:
        copy.start()
    for b in range(blocks):
        at = b * BLOCK
        entering = attn_ref[length + b * HEAD_DIM : length + (b + 1) * HEAD_DIM, :]
        for i in range(BLOCK // TILE):
            rows = slice(at + i * TILE, at + (i + 1) * TILE)
            cols = slice(at, at + (i + 1) * TILE)
            q, g = q_ref[rows, :], grad_ref[rows, :]
            table = table_ref[rows, : (i + 1) * TILE]
            gw = (dot(g, v_ref[cols, :], 1, 1) * table).astype(bf16)
            grad_q = dot(gw, k_ref[cols, :]) + front_ref[rows, :] * exact_dot(g, entering, True)
            gq_ref[rows, :] = grad_q.astype(bf16)
            add_k = dot(gw, q, 0, 0)
            more_k = base_k_ref[rows, :] if b < blocks - 1 else 0.0
            if i:
                old = slice(at, at + i * TILE)
                gk_ref[old, :] += add_k[: i * TILE, :]
            gk_ref[rows, :] = add_k[i * TILE :, :] + more_k
    for copy in copies:
        copy.wait()


def finish_kernel(
    k_ref, v_ref, gk_ref, gv_ref, keep_ref, got_ref, sums_ref, tail_ref, gq_ref,
    ok_hbm, ov_hbm, oq_hbm, ok_ref, ov_ref, sems,
):
    length = k_ref.shape[0]
    blocks = length // BLOCK
    sums = sums_ref[...]
    start = whole_state(keep_ref, got_ref)
    after = jnp.zeros((1, 1), f32)
    copies = [pltpu.make_async_copy(gq_ref, oq_hbm, sems.at[2 * blocks])]
    copies[0].start()
    for b in reversed(range(blocks)):
        at = b * BLOCK
        rows = slice(at, at + BLOCK)
        tail = tail_ref[rows, :]
        state = start * jnp.exp(after)
        after = after + last_of(sums, b)
        part = pl.ds(at, BLOCK)
        ok_ref[rows, :] = (gk_ref[rows, :] + tail * exact_dot(v_ref[rows, :], state, True)).astype(bf16)
        copies.append(pltpu.make_async_copy(ok_ref.at[part], ok_hbm.at[part], sems.at[2 * b]))
        copies[-1].start()
        ov_ref[rows, :] = (gv_ref[rows, :] + tail * exact_dot(k_ref[rows, :], state)).astype(bf16)
        copies.append(pltpu.make_async_copy(ov_ref.at[part], ov_hbm.at[part], sems.at[2 * b + 1]))
        copies[-1].start()
    for copy in copies:
        copy.wait()


def call(kernel, name, out, *args, cost=2e6, hbm_in=False, hbm_last=False, hbm_out=0, scratch=()):
    shapes = [jax.ShapeDtypeStruct(s, d) for s, d in out]
    places = [pltpu.HBM if hbm_in else pltpu.VMEM] * len(args)
    if hbm_last:
        places[-1] = pl.ANY
    place_out = [pltpu.HBM] * hbm_out + [pltpu.VMEM] * (len(out) - hbm_out)
    return pl.pallas_call(
        kernel,
        out_shape=shapes,
        in_specs=[pl.BlockSpec(memory_space=place) for place in places],
        out_specs=[pl.BlockSpec(memory_space=place) for place in place_out],
        scratch_shapes=scratch,
        compiler_params=pltpu.CompilerParams(vmem_limit_bytes=16 << 20),
        cost_estimate=pl.CostEstimate(flops=int(cost), bytes_accessed=int(cost), transcendentals=0),
        name=name,
    )(*args)


def exchange(x, axis, groups=None):
    return lax.all_to_all(x, axis, 0, 0, axis_index_groups=groups)


def on_device(queries, key_rows, value_rows, gate_input, norm_gain, log_decay, grad_output):
    length = queries.shape[0]
    n_ctx, n_exp, n_section = (lax.axis_size(a) for a in ("ctx", "exp", "section"))
    n_chip = n_ctx // 2
    width = HEAD_DIM * n_exp * n_section
    blocks = length // BLOCK
    chunks = length // CHUNK
    part = HEAD_DIM // 2
    pairs = [(i, i ^ 1) for i in range(n_ctx)]
    lines = [[2 * i + core for i in range(n_chip)] for core in range(2)]
    rates = log_decay.reshape(chunks, CHUNK)
    full, half = ((length, HEAD_DIM), f32), ((length, HEAD_DIM), bf16)
    piece, marked = ((part, HEAD_DIM), f32), ((part + 8, HEAD_DIM), f32)

    sent, keep, entry, sums, turned, gain, held_k, held_v, held_q = call(
        states_kernel, "states",
        [marked, marked, ((blocks - 1, HEAD_DIM, HEAD_DIM), f32), ((chunks, CHUNK), f32),
         ((CHUNK, 4 * chunks), f32), ((1, HEAD_DIM), f32), half, half, half],
        *(
            pltpu.with_memory_space_constraint(a, pltpu.HBM)
            for a in (key_rows, value_rows, queries, rates, norm_gain.reshape(1, HEAD_DIM))
        ),
        hbm_in=True, cost=1e7,
        scratch=[
            pltpu.VMEM((chunks, CHUNK), f32), pltpu.VMEM((HEAD_DIM, HEAD_DIM), f32),
            pltpu.SemaphoreType.DMA((2 * blocks + 3,)),
        ],
    )
    got = lax.ppermute(sent, "ctx", pairs)
    local, table, weights = call(
        local_kernel, "local", [full, ((length, BLOCK), f32), ((length, BLOCK), bf16)],
        held_q, held_k, held_v, sums, turned,
    )
    sent, first, totals = call(
        partial(pair_kernel, n_chip), "pair",
        [((n_chip, part + 8, HEAD_DIM), f32), piece, ((16, HEAD_DIM), f32)],
        keep, got, local, hbm_last=True,
    )
    got = exchange(sent, "ctx", lines)
    signal, fronted, front = call(
        gate_kernel, "gate", [full, ((3 * HEAD_DIM, length), bf16), full],
        gate_input, grad_output, gain, held_q, sums, turned,
    )
    keep, sent, chips = call(
        partial(prefix_kernel, n_chip), "prefix", [piece, piece, ((n_chip, HEAD_DIM), f32)],
        got, first, totals,
    )
    got = lax.ppermute(sent, "ctx", pairs)
    attn, sent = call(
        partial(attn_kernel, n_section), "attn",
        [((length + blocks * HEAD_DIM, HEAD_DIM), f32), ((n_section, 16, CHUNK), f32)],
        held_q, local, keep, got, entry, sums, front, signal,
    )
    got = exchange(sent, "section")
    (sent,) = call(
        partial(relay_kernel, n_section, n_exp), "relay", [((n_exp, 16, CHUNK), f32)], got
    )
    got = exchange(sent, "exp")
    grad, keep, sent, aux = call(
        partial(grad_kernel, n_exp, width), "grad",
        [half, piece, piece, ((blocks * HEAD_DIM, HEAD_DIM), f32)],
        got, attn, signal, fronted, sums,
        scratch=[pltpu.VMEM((HEAD_DIM, HEAD_DIM), f32)],
    )
    got = lax.ppermute(sent, "ctx", pairs)
    early = ((length - BLOCK, HEAD_DIM), f32)
    layer_out, grad_gate, base_k, local_v, tail = call(
        output_kernel, "output", [half, half, early, full, full],
        attn, aux, gate_input, gain, grad_output, held_k, held_v, turned, weights, grad,
    )
    sent, second = call(
        partial(back_pair_kernel, n_chip), "back_pair",
        [((n_chip, part, HEAD_DIM), f32), piece], keep, got, totals, base_k, hbm_last=True,
    )
    got = exchange(sent, "ctx", lines)
    layer_out, grad_gate, grad_q, local_k = call(
        backward_kernel, "backward", [half, half, half, full],
        held_q, held_k, held_v, grad, attn, base_k, table, front,
        layer_out, grad_gate, hbm_out=2, scratch=[pltpu.SemaphoreType.DMA((2,))],
    )
    keep, sent = call(
        partial(suffix_kernel, n_chip), "suffix", [piece, piece], got, second, totals, chips
    )
    got = lax.ppermute(sent, "ctx", pairs)
    grad_k, grad_v, grad_q = call(
        finish_kernel, "finish", [half, half, half],
        held_k, held_v, local_k, local_v, keep, got, sums, tail, grad_q, hbm_out=3,
        scratch=[
            pltpu.VMEM((length, HEAD_DIM), bf16), pltpu.VMEM((length, HEAD_DIM), bf16),
            pltpu.SemaphoreType.DMA((2 * blocks + 1,)),
        ],
    )
    return layer_out, grad_q, grad_k, grad_v, grad_gate


def solution(mesh):
    block = P("ctx", ("section", "exp"))
    in_specs = (
        block, block, block, block, P(("section", "exp")), P(("section", "exp"), "ctx"), block,
    )
    return jax.shard_map(
        on_device, mesh=mesh, in_specs=in_specs, out_specs=(block,) * 5, check_vma=False
    )
```
